32 devices in a mesh: dp: 8 (over z, y), sp: 4 (over x, core).
Axes of the slice: x: 2, y: 2, z: 4, core: 2. Of those that a mesh axis runs over, the one named last changes fastest.
Arguments:
- layer_input: bfloat16 [8, 512, 8192], P('dp', 'sp'), may hold values from -6 to 6
- value_weight: bfloat16 [8192, 512], P(('dp', 'sp')), may hold values from -0.0625 to 0.0625
- query_states: bfloat16 [8, 512, 4096], P('dp', 'sp'), may hold values from -40 to 40, as said below
- key_states: bfloat16 [8, 512, 512], P('dp', 'sp'), may hold values from -5 to 5
- out_grad: bfloat16 [8, 512, 4096], P('dp', 'sp'), may hold values from -6 to 6
- doc_ids: int32 [8, 512], P('dp', 'sp'), may hold values from 0 to 3, never falling along the last dimension, each value on 1 to 256 neighbouring positions
Outputs:
- query_grad: bfloat16 [8, 512, 4096], P('dp', 'sp')
- key_grad: bfloat16 [8, 512, 512], P('dp', 'sp')
- input_grad: bfloat16 [8, 512, 8192], P('dp', 'sp')
- value_weight_grad: float32 [8192, 512], P(('dp', 'sp'))
The draws below stay inside these ranges and needn't reach their ends.
Inputs may be any that keep to these rules, and one draw needn't show every extreme that they name: `query_states`: queries of a head may be large multiples of keys of the same positions.
All inputs are finite; a program needn't handle non-finite values.
Results may differ from the reference program's by a relative error of at most 0.0085.
Values may be sent and summed in bfloat16 or wider, within the bound.
No kernel may reach another device: no remote copies, remote signals or barrier semaphores. Data moves between devices by JAX's collectives and lax.ppermute only.
A program may use at most 128 MiB of HBM per device.

```python
import math
import jax
import jax.numpy as jnp
import numpy as np
from jax import lax

D = 8192
H = 32
KVH = 4
HD = 128
DOCS = 4
SEQS = 8
LEN = 512


def shared_keys(key):
    base_key = jax.random.fold_in(key, 7)
    key_vals = jnp.clip(jax.random.normal(base_key, (SEQS, LEN, KVH * HD), jnp.float32), -5.0, 5.0)
    return key_vals


def draw_key_states(key, part):
    key_vals = shared_keys(key)
    return key_vals.astype(jnp.bfloat16)


def draw_query_states(key, part):
    own_key = jax.random.fold_in(key, 11)
    query_vals = jnp.clip(jax.random.normal(own_key, (SEQS, LEN, H * HD), jnp.float32), -5.0, 5.0)
    return query_vals.astype(jnp.bfloat16)


def spiked(result, key, source, target, blocks, factor):
    owner, partner = [(jnp.arange(result.shape[axis_at]) // (result.shape[axis_at] // blocks)).reshape([-1 if axis == axis_at else 1 for axis in range(result.ndim)]) for axis_at in (source, target)]
    chosen = jax.random.permutation(key, blocks)[partner]
    strong = (owner == chosen) | (owner == (partner + blocks // 2) % blocks)
    return jnp.where(strong, factor * result, result)


def steps_of(key, extent, split, low, top_value):
    level, own = 1.0, jax.random.fold_in(key, 6)
    for dim, parts in split:
        draws = jnp.exp(jax.random.uniform(jax.random.fold_in(own, dim), (parts,), jnp.float32, low / len(split), top_value / len(split)))
        level = level * jnp.repeat(draws, extent[dim] // parts).reshape([-1 if axis == dim else 1 for axis in range(len(extent))])
    return level


def profile(amount, total, bound, lean):
    weights = [(1 << 20) // math.isqrt(standing ** lean) + 1 for standing in range(2, amount + 1)]
    spare, counts = total - bound - (amount - 1), [1] * (amount - 1)
    while spare > 0:
        free = [i for i in range(amount - 1) if counts[i] < bound]
        pool, budget = sum([weights[i] for i in free]), spare
        for i in free:
            extra = min(bound - counts[i], max(1, budget * weights[i] // pool), spare)
            counts[i] = counts[i] + extra
            spare = spare - extra
    return np.array([bound] + counts)


def ragged(key, number_of, total, reach, skew):
    if number_of == 2:
        one = jax.random.randint(key, (), max(1, total - reach), min(reach, total - 1) + 1)
        return jnp.stack([one, total - one])
    sizes = jnp.asarray(profile(number_of, total, reach, skew), jnp.int32)
    pairs = (number_of - 1) // 2
    source_of, taker = sizes[1:1 + 2 * pairs:2], sizes[2:2 + 2 * pairs:2]
    slack = jnp.minimum(source_of - 1, reach - taker)
    passed = jax.random.randint(jax.random.fold_in(key, 1), (pairs,), 0, 1 << 20) % (slack + 1)
    sizes = sizes.at[1:1 + 2 * pairs:2].set(source_of - passed).at[2:2 + 2 * pairs:2].set(taker + passed)
    return sizes[jax.random.permutation(jax.random.fold_in(key, 2), number_of)]


def bell_draw(key, extent, spread, most, shards=(), dtype=jnp.bfloat16):
    values = jax.random.normal(key, extent, jnp.float32) * spread
    if len(shards) > 0:
        values = steps_of(key, extent, shards, -0.22, 0.18) * values
    return jnp.clip(values, min=-most, max=most).astype(dtype)


def gaussian_with(key, dims, width, limit, cuts, heavy, held_as=jnp.bfloat16):
    drawn = width * jax.random.normal(key, dims, jnp.float32)
    if cuts:
        drawn = drawn * steps_of(key, dims, cuts, -0.22, 0.18)
    return jnp.clip(spiked(drawn, jax.random.fold_in(key, 3), *heavy), -limit, limit).astype(held_as)


def setup_inputs(seed: int = 0) -> dict:
    streams_of = jax.random.split(jax.random.key(seed), 7)
    return {
        "layer_input": gaussian_with(streams_of[0], (SEQS, LEN, D), 1.0, 6.0, ((0, 8), (1, 4)), (1, 2, 4, 2.0)),
        "value_weight": bell_draw(streams_of[1], (D, KVH * HD), D ** -0.5, 0.0625, ((0, 32),)),
        "query_states": draw_query_states(jax.random.fold_in(streams_of[6], 71), 0),
        "key_states": draw_key_states(jax.random.fold_in(streams_of[6], 71), 0),
        "out_grad": bell_draw(streams_of[4], (SEQS, LEN, H * HD), 1.0, 6.0, ((0, 8), (1, 4))),
        "doc_ids": jax.vmap(lambda own: jnp.searchsorted(jnp.cumsum(ragged(own, DOCS, LEN, LEN // 2, 0)), jnp.arange(LEN), side="right"))(jax.random.split(streams_of[5], SEQS)).reshape((SEQS, LEN)).astype(jnp.int32),
    }


def group_grads(q_group, g_group, k_single, v_single, seg_ids):
    scale_f = HD ** -0.5
    q_full = q_group.astype(jnp.float32)
    g_full = g_group.astype(jnp.float32)
    k_full = k_single.astype(jnp.float32)
    v_full = v_single.astype(jnp.float32)
    scores = jnp.einsum('qhd,kd->hqk', q_full, k_full) * scale_f
    places = jnp.arange(LEN)
    allowed = (places[None, :] <= places[:, None]) & (seg_ids[:, None] == seg_ids[None, :])
    scores = jnp.where(allowed[None], scores, jnp.float32(-1e30))
    row_max = jnp.max(scores, axis=-1, keepdims=True)
    expons = jnp.exp(scores - row_max)
    probs = expons / jnp.sum(expons, axis=-1, keepdims=True)
    dprobs = jnp.einsum('qhd,kd->hqk', g_full, v_full)
    deltas = jnp.sum(probs * dprobs, axis=-1, keepdims=True)
    dscores = (probs * (dprobs - deltas) * scale_f).astype(jnp.bfloat16).astype(jnp.float32)
    probs_bf = probs.astype(jnp.bfloat16).astype(jnp.float32)
    query_g = jnp.einsum('hqk,kd->qhd', dscores, k_full).astype(jnp.bfloat16)
    key_g = jnp.einsum('hqk,qhd->kd', dscores, q_full).astype(jnp.bfloat16)
    value_g = jnp.einsum('hqk,qhd->kd', probs_bf, g_full).astype(jnp.bfloat16)
    return query_g, key_g, value_g


def sequence_grads(pieces):
    q_seq, g_seq, k_seq, v_seq, seg_ids = pieces
    group_size = H // KVH
    q_heads = q_seq.reshape(LEN, KVH, group_size, HD).transpose(1, 0, 2, 3)
    g_heads = g_seq.reshape(LEN, KVH, group_size, HD).transpose(1, 0, 2, 3)
    k_heads = k_seq.reshape(LEN, KVH, HD).transpose(1, 0, 2)
    v_heads = v_seq.reshape(LEN, KVH, HD).transpose(1, 0, 2)

    def one_group(items):
        return group_grads(items[0], items[1], items[2], items[3], seg_ids)

    query_g, key_g, value_g = lax.map(one_group, (q_heads, g_heads, k_heads, v_heads))
    query_g = query_g.transpose(1, 0, 2, 3).reshape(LEN, H * HD)
    key_g = key_g.transpose(1, 0, 2).reshape(LEN, KVH * HD)
    value_g = value_g.transpose(1, 0, 2).reshape(LEN, KVH * HD)
    return query_g, key_g, value_g


def reference(layer_input, value_weight, query_states, key_states, out_grad, doc_ids):
    flat_input = layer_input.reshape(SEQS * LEN, D)
    values = jnp.dot(flat_input, value_weight, preferred_element_type=jnp.float32).astype(jnp.bfloat16)
    values = values.reshape(SEQS, LEN, KVH * HD)
    query_grad, key_grad, value_grad = lax.map(sequence_grads, (query_states, out_grad, key_states, values, doc_ids))
    flat_vgrad = value_grad.reshape(SEQS * LEN, KVH * HD)
    input_grad = lax.dot_general(flat_vgrad, value_weight, (((1,), (1,)), ((), ())), preferred_element_type=jnp.float32)
    input_grad = input_grad.astype(jnp.bfloat16).reshape(SEQS, LEN, D)
    weight_grad = lax.dot_general(flat_input, flat_vgrad, (((0,), (0,)), ((), ())), preferred_element_type=jnp.float32)
    return (query_grad, key_grad, input_grad, weight_grad)
```

```python
import functools
import math

import jax
import jax.numpy as jnp
import numpy as np
from jax import lax
from jax.experimental import pallas as pl
from jax.experimental.pallas import tpu as pltpu
from jax.sharding import PartitionSpec as P

HD = 128
NEG = -1e30
BF = jnp.bfloat16
F32 = jnp.float32
NT = (((1,), (1,)), ((), ()))
TN = (((0,), (0,)), ((), ()))
NN = (((1,), (0,)), ((), ()))
LIMIT = 60 * 1024 * 1024


def dot(a, b, dims):
    return lax.dot_general(a, b, dims, preferred_element_type=F32)


def ring_order(count):
    return list(range(0, count, 2)) + list(range(1, count, 2))[::-1]


def rows_at(index, size):
    return pl.ds(pl.multiple_of(index * size, size), size)


def whole(shape):
    return pl.BlockSpec(shape, lambda *_: (0,) * len(shape))


def split_kernel(sp, reps, width, idx_ref, x_ref, *rest):
    outs, hold = rest[:sp], rest[sp]
    for a in range(sp):
        for d in range(reps):
            hold[a, :, d * width : (d + 1) * width] = x_ref[
                :, (d * sp + a) * width : (d * sp + a + 1) * width
            ]
    for r in range(sp):
        outs[r][...] = hold[idx_ref[r]]


def split_columns(x, fwd, sp, dp, width):
    tok = x.shape[0]
    reps = max(1, 128 // width)
    block = reps * width
    return pl.pallas_call(
        functools.partial(split_kernel, sp, reps, width),
        out_shape=[jax.ShapeDtypeStruct((tok, dp * width), BF)] * sp,
        grid_spec=pltpu.PrefetchScalarGridSpec(
            num_scalar_prefetch=1,
            grid=(dp // reps,),
            in_specs=[pl.BlockSpec((tok, sp * block), lambda d, _: (0, d))],
            out_specs=[pl.BlockSpec((tok, block), lambda d, _: (0, d))] * sp,
            scratch_shapes=[pltpu.VMEM((sp, tok, block), BF)],
        ),
        compiler_params=pltpu.CompilerParams(vmem_limit_bytes=LIMIT),
        cost_estimate=pl.CostEstimate(
            flops=0, bytes_accessed=4 * x.size, transcendentals=0
        ),
        name="split_columns",
    )(fwd, x)


def join_kernel(sp, reps, width, idx_ref, *rest):
    ins, out, hold = rest[:sp], rest[sp], rest[sp + 1]
    for r in range(sp):
        hold[idx_ref[r]] = ins[r][...]
    for a in range(sp):
        for d in range(reps):
            out[:, (d * sp + a) * width : (d * sp + a + 1) * width] = hold[
                a, :, d * width : (d + 1) * width
            ]


def join_columns(pieces, fwd, sp, dp, width):
    tok = pieces[0].shape[0]
    reps = max(1, 128 // width)
    block = reps * width
    return pl.pallas_call(
        functools.partial(join_kernel, sp, reps, width),
        out_shape=jax.ShapeDtypeStruct((tok, sp * dp * width), BF),
        grid_spec=pltpu.PrefetchScalarGridSpec(
            num_scalar_prefetch=1,
            grid=(dp // reps,),
            in_specs=[pl.BlockSpec((tok, block), lambda d, _: (0, d))] * sp,
            out_specs=pl.BlockSpec((tok, sp * block), lambda d, _: (0, d)),
            scratch_shapes=[pltpu.VMEM((sp, tok, block), BF)],
        ),
        compiler_params=pltpu.CompilerParams(vmem_limit_bytes=LIMIT),
        cost_estimate=pl.CostEstimate(
            flops=0, bytes_accessed=4 * tok * sp * dp * width, transcendentals=0
        ),
        name="join_columns",
    )(fwd, *pieces)


def fill_keys(sp, tok, win, heads, idx_ref, kd_refs, key_hold, doc_hold, bias):
    first = jnp.maximum(idx_ref[0] + 1 - win, 0)
    for r in range(sp):
        key_hold[rows_at(idx_ref[r], tok), :] = kd_refs[r][0:tok, :]

    @pl.when(pl.program_id(0) == 0)
    def _():
        for r in range(sp):
            doc_hold[idx_ref[r]] = kd_refs[r][tok : tok + 16, 0:tok].astype(F32)
        own = jnp.broadcast_to(doc_hold[idx_ref[0]][0:1, :], (tok, tok))
        query_at = idx_ref[0] * tok + lax.broadcasted_iota(jnp.int32, (tok, tok), 1)
        for b in range(win):
            docs = jnp.broadcast_to(doc_hold[first + b][0:1, :], (tok, tok)).T
            key_at = (first + b) * tok + lax.broadcasted_iota(jnp.int32, (tok, tok), 0)
            ok = (key_at <= query_at) & (docs == own)
            block = jnp.where(ok, F32(0.0), F32(NEG))
            for h in range(heads):
                bias[b * tok : (b + 1) * tok, h * tok : (h + 1) * tok] = block

    return first


def stack_heads(src, dst, tok, group):
    for h in range(group):
        dst[h * tok : (h + 1) * tok, :] = src[:, h * HD : (h + 1) * HD]


def emit_rel(acc, first, value, sp, nx, tok, win, idx_ref, keep, send):
    acc[...] = jnp.zeros_like(acc)
    acc[pl.ds(pl.multiple_of(first * tok, tok), win * tok), :] = value
    for dx in range(nx):
        keep[dx] = acc[rows_at(idx_ref[dx], tok), :]
        send[dx] = acc[rows_at(idx_ref[nx + dx], tok), :]


def probs_kernel(sp, tok, win, group, pair, idx_ref, q_ref, g_ref, *rest):
    nx = sp // 2
    kds, (keep, send, lse_ref) = rest[:sp], rest[sp : sp + 3]
    key_hold, doc_hold, bias, q_st, g_st, p_st, acc = rest[sp + 3 :]
    first = fill_keys(sp, tok, win, pair, idx_ref, kds, key_hold, doc_hold, bias)
    factor = F32(HD**-0.5 * math.log2(math.e))
    stack_heads(q_ref, q_st, tok, group)
    stack_heads(g_ref, g_st, tok, group)
    keys = key_hold[pl.ds(pl.multiple_of(first * tok, tok), win * tok), :]
    for h in range(0, group, pair):
        at = slice(h * tok, (h + pair) * tok)
        s = dot(keys, q_st[at, :], NT) * factor + bias[...]
        top = jnp.max(s, axis=0, keepdims=True)
        e = jnp.exp2(s - top)
        total = jnp.sum(e, axis=0, keepdims=True)
        p_st[:, at] = (e * (1.0 / total)).astype(BF)
        lse = top + jnp.log2(total)
        for i in range(pair):
            lse_ref[h + i : h + i + 1, :] = lse[:, i * tok : (i + 1) * tok]
    emit_rel(
        acc, first, dot(p_st[...], g_st[...], NN), sp, nx, tok, win, idx_ref, keep, send
    )


def probs_call(idx, q, g, kds, sp, tok, win, kvh, group):
    nx, seq, pair = sp // 2, sp * tok, 2
    part = jax.ShapeDtypeStruct((nx, tok, kvh * HD), F32)
    part_spec = pl.BlockSpec((nx, tok, HD), lambda c, _: (0, 0, c))
    wide = pl.BlockSpec((tok, group * HD), lambda c, _: (0, c))
    return pl.pallas_call(
        functools.partial(probs_kernel, sp, tok, win, group, pair),
        out_shape=[part, part, jax.ShapeDtypeStruct((kvh * group, tok), F32)],
        grid_spec=pltpu.PrefetchScalarGridSpec(
            num_scalar_prefetch=1,
            grid=(kvh,),
            in_specs=[wide, wide]
            + [pl.BlockSpec((tok + 16, HD), lambda c, _: (0, c))] * sp,
            out_specs=[part_spec, part_spec, pl.BlockSpec((group, tok), lambda c, _: (c, 0))],
            scratch_shapes=[
                pltpu.VMEM((seq, HD), BF),
                pltpu.VMEM((sp, 16, tok), F32),
                pltpu.VMEM((win * tok, pair * tok), F32),
                pltpu.VMEM((group * tok, HD), BF),
                pltpu.VMEM((group * tok, HD), BF),
                pltpu.VMEM((win * tok, group * tok), BF),
                pltpu.VMEM((seq, HD), F32),
            ],
        ),
        compiler_params=pltpu.CompilerParams(vmem_limit_bytes=LIMIT),
        cost_estimate=pl.CostEstimate(
            flops=4 * tok * win * tok * kvh * group * HD,
            bytes_accessed=8 * 1024 * 1024,
            transcendentals=tok * win * tok * kvh * group,
        ),
        name="probs_dv",
    )(idx, q, g, *kds)


def scores_kernel(sp, tok, win, group, pair, idx_ref, q_ref, g_ref, lse_ref, v0_ref, v1_ref, *rest):
    nx = sp // 2
    kds, (dq_ref, keep, send) = rest[:sp], rest[sp : sp + 3]
    key_hold, doc_hold, bias, val_hold, q_st, g_st, ds_st, acc = rest[sp + 3 :]
    first = fill_keys(sp, tok, win, pair, idx_ref, kds, key_hold, doc_hold, bias)
    for dx in range(nx):
        val_hold[rows_at(idx_ref[dx], tok), :] = v0_ref[dx]
        val_hold[rows_at(idx_ref[nx + dx], tok), :] = v1_ref[dx]
    scale = HD**-0.5
    factor = F32(scale * math.log2(math.e))
    stack_heads(q_ref, q_st, tok, group)
    stack_heads(g_ref, g_st, tok, group)
    window = pl.ds(pl.multiple_of(first * tok, tok), win * tok)
    keys, vals = key_hold[window, :], val_hold[window, :]
    for h in range(0, group, pair):
        at = slice(h * tok, (h + pair) * tok)
        lse = jnp.concatenate([lse_ref[h + i : h + i + 1, :] for i in range(pair)], axis=1)
        shift = lse - F32(math.log2(scale))
        s = dot(keys, q_st[at, :], NT) * factor + bias[...]
        scaled = jnp.exp2(s - shift)
        dp = dot(vals, g_st[at, :], NT)
        delta = jnp.sum(scaled * dp, axis=0, keepdims=True) * F32(1.0 / scale)
        ds_st[:, at] = (scaled * (dp - delta)).astype(BF)
    dq = dot(ds_st[...], keys, TN)
    for h in range(group):
        dq_ref[:, h * HD : (h + 1) * HD] = dq[h * tok : (h + 1) * tok, :].astype(BF)
    emit_rel(
        acc, first, dot(ds_st[...], q_st[...], NN), sp, nx, tok, win, idx_ref, keep, send
    )


def scores_call(idx, q, g, lse, v0, v1, kds, sp, tok, win, kvh, group):
    nx, seq, pair = sp // 2, sp * tok, 2
    part = jax.ShapeDtypeStruct((nx, tok, kvh * HD), F32)
    part_spec = pl.BlockSpec((nx, tok, HD), lambda c, _: (0, 0, c))
    wide = pl.BlockSpec((tok, group * HD), lambda c, _: (0, c))
    return pl.pallas_call(
        functools.partial(scores_kernel, sp, tok, win, group, pair),
        out_shape=[jax.ShapeDtypeStruct(q.shape, BF), part, part],
        grid_spec=pltpu.PrefetchScalarGridSpec(
            num_scalar_prefetch=1,
            grid=(kvh,),
            in_specs=[wide, wide, pl.BlockSpec((group, tok), lambda c, _: (c, 0)), part_spec, part_spec]
            + [pl.BlockSpec((tok + 16, HD), lambda c, _: (0, c))] * sp,
            out_specs=[wide, part_spec, part_spec],
            scratch_shapes=[
                pltpu.VMEM((seq, HD), BF),
                pltpu.VMEM((sp, 16, tok), F32),
                pltpu.VMEM((win * tok, pair * tok), F32),
                pltpu.VMEM((seq, HD), BF),
                pltpu.VMEM((group * tok, HD), BF),
                pltpu.VMEM((group * tok, HD), BF),
                pltpu.VMEM((win * tok, group * tok), BF),
                pltpu.VMEM((seq, HD), F32),
            ],
        ),
        compiler_params=pltpu.CompilerParams(vmem_limit_bytes=LIMIT),
        cost_estimate=pl.CostEstimate(
            flops=8 * tok * win * tok * kvh * group * HD,
            bytes_accessed=10 * 1024 * 1024,
            transcendentals=tok * win * tok * kvh * group,
        ),
        name="scores_dq_dk",
    )(idx, q, g, lse, v0, v1, *kds)


def values_kernel(sp, dp, tok, width, idx_ref, *rest):
    nx = sp // 2
    xs, ws = rest[:sp], rest[sp : sp + dp]
    keep, send, w_out = rest[sp + dp :]
    for i in range(dp):
        w_out[rows_at(idx_ref[i], width), :] = ws[i][...]
    for dx in range(nx):
        keep[dx] = dot(xs[dx][...], w_out[...], NN)
        send[dx] = dot(xs[nx + dx][...], w_out[...], NN)


def values_call(idx, xs, ws, sp, dp, tok, width):
    nx, kv = sp // 2, ws[0].shape[1]
    cols = dp * width
    part = jax.ShapeDtypeStruct((nx, tok, kv), F32)
    return pl.pallas_call(
        functools.partial(values_kernel, sp, dp, tok, width),
        out_shape=[part, part, jax.ShapeDtypeStruct((cols, kv), BF)],
        grid_spec=pltpu.PrefetchScalarGridSpec(
            num_scalar_prefetch=1,
            grid=(1,),
            in_specs=[whole((tok, cols))] * sp + [whole((width, kv))] * dp,
            out_specs=[whole((nx, tok, kv))] * 2 + [whole((cols, kv))],
        ),
        compiler_params=pltpu.CompilerParams(vmem_limit_bytes=LIMIT),
        cost_estimate=pl.CostEstimate(
            flops=2 * sp * tok * cols * kv, bytes_accessed=8 * 1024 * 1024, transcendentals=0
        ),
        name="values_part",
    )(idx, *xs, *ws)


def wgrad_kernel(sp, nz, ny, tok, width, idx_ref, *rest):
    nx = sp // 2
    xs, (g0, g1) = rest[:sp], rest[sp : sp + 2]
    outs = rest[sp + 2 : sp + 2 + 2 * nz]
    x_hold, g_hold, total = rest[sp + 2 + 2 * nz :]
    for dx in range(nx):
        for core, src in ((0, g0), (1, g1)):
            r = core * nx + dx
            x_hold[r * tok : (r + 1) * tok, :] = xs[r][...]
            g_hold[r * tok : (r + 1) * tok, :] = src[dx]
    cols = x_hold.shape[1]
    step = min(cols, 512)
    for at in range(0, cols, step):
        total[at : at + step, :] = dot(x_hold[:, at : at + step], g_hold[...], TN)
    for k in range(nz):
        outs[k][...] = total[rows_at(idx_ref[k * ny], width), :].astype(BF)
        for j in range(1, ny):
            outs[nz + k][j - 1] = total[rows_at(idx_ref[k * ny + j], width), :]


def wgrad_call(idx, xs, g0, g1, sp, nz, ny, tok, width):
    nx, kv = sp // 2, g0.shape[2]
    cols = nz * ny * width
    return pl.pallas_call(
        functools.partial(wgrad_kernel, sp, nz, ny, tok, width),
        out_shape=[jax.ShapeDtypeStruct((width, kv), BF)] * nz
        + [jax.ShapeDtypeStruct((ny - 1, width, kv), F32)] * nz,
        grid_spec=pltpu.PrefetchScalarGridSpec(
            num_scalar_prefetch=1,
            grid=(1,),
            in_specs=[whole((tok, cols))] * sp + [whole((nx, tok, kv))] * 2,
            out_specs=[whole((width, kv))] * nz + [whole((ny - 1, width, kv))] * nz,
            scratch_shapes=[
                pltpu.VMEM((sp * tok, cols), BF),
                pltpu.VMEM((sp * tok, kv), BF),
                pltpu.VMEM((cols, kv), F32),
            ],
        ),
        compiler_params=pltpu.CompilerParams(vmem_limit_bytes=LIMIT),
        cost_estimate=pl.CostEstimate(
            flops=2 * sp * tok * cols * kv, bytes_accessed=7 * 1024 * 1024, transcendentals=0
        ),
        name="weight_grad_part",
    )(idx, *xs, g0, g1)


def igrad_kernel(sp, g0, g1, w_ref, *outs):
    nx = sp // 2
    for dx in range(nx):
        outs[dx][...] = dot(g0[dx], w_ref[...], NT).astype(BF)
        outs[nx + dx][...] = dot(g1[dx], w_ref[...], NT).astype(BF)


def igrad_call(g0, g1, w, sp, tok):
    nx, kv = sp // 2, g0.shape[2]
    cols = w.shape[0]
    return pl.pallas_call(
        functools.partial(igrad_kernel, sp),
        out_shape=[jax.ShapeDtypeStruct((tok, cols), BF)] * sp,
        grid=(1,),
        in_specs=[whole((nx, tok, kv))] * 2 + [whole((cols, kv))],
        out_specs=[whole((tok, cols))] * sp,
        compiler_params=pltpu.CompilerParams(vmem_limit_bytes=LIMIT),
        cost_estimate=pl.CostEstimate(
            flops=2 * sp * tok * cols * kv, bytes_accessed=5 * 1024 * 1024, transcendentals=0
        ),
        name="input_grad_part",
    )(g0, g1, w)


def local(layer_input, value_weight, query_states, key_states, out_grad, doc_ids):
    sp, dp = lax.axis_size("sp"), lax.axis_size("dp")
    nx = sp // 2
    ny = max(1, min(nx, dp))
    nz = dp // ny
    tok = layer_input.shape[1]
    width = value_weight.shape[0]
    kvh = key_states.shape[2] // HD
    group = query_states.shape[2] // HD // kvh
    win = min(sp, sp // 2 + 1)
    s, d = lax.axis_index("sp"), lax.axis_index("dp")
    x_at, core = s // 2, s % 2
    z_at, y_at = d // ny, d % ny

    def sp_perm(dx, dc):
        return [(i, ((i // 2 + dx) % nx) * 2 + (i % 2 ^ dc)) for i in range(sp)]

    def send_sp(v, dx, dc):
        return lax.ppermute(v, "sp", sp_perm(dx % nx, dc))

    z_ring, y_ring = ring_order(nz), ring_order(ny)

    def pred(ring, at, k):
        table = np.zeros(len(ring), np.int32)
        for p, v in enumerate(ring):
            table[v] = ring[(p - k) % len(ring)]
        return jnp.asarray(table)[at]

    z_next = [
        (z_ring[p] * ny + y, z_ring[(p + 1) % nz] * ny + y) for p in range(nz) for y in range(ny)
    ]
    y_next = [
        (z * ny + y_ring[p], z * ny + y_ring[(p + 1) % ny]) for p in range(ny) for z in range(nz)
    ]

    def block_of(k, j):
        return pred(z_ring, z_at, k) * ny + pred(y_ring, y_at, j)

    rel = jnp.stack(
        [((x_at - dx) % nx) * 2 + (core ^ dc) for dc in range(2) for dx in range(nx)]
    ).astype(jnp.int32)
    fwd = jnp.stack(
        [((x_at + dx) % nx) * 2 + (core ^ dc) for dc in range(2) for dx in range(nx)]
    ).astype(jnp.int32)
    gather_at = jnp.stack([block_of(k, j) for k in range(nz) for j in range(ny)]).astype(jnp.int32)
    scatter_at = jnp.stack(
        [block_of(k, j) for k in range(1, nz + 1) for j in range(1, ny + 1)]
    ).astype(jnp.int32)

    doc_rows = jnp.pad(
        jnp.broadcast_to(doc_ids.astype(BF), (16, tok)), ((0, 0), (0, kvh * HD - tok))
    )
    kd = jnp.concatenate([key_states[0], doc_rows], axis=0)
    near = [kd] + [send_sp(kd, dx, 0) for dx in range(1, nx)]
    kds = near + [send_sp(v, 0, 1) for v in near]

    rows = []
    at_z = value_weight
    for k in range(nz):
        at_y = at_z
        for j in range(ny):
            rows.append(at_y)
            if j + 1 < ny:
                at_y = lax.ppermute(at_y, "dp", y_next)
        if k + 1 < nz:
            at_z = lax.ppermute(at_z, "dp", z_next)

    pieces = split_columns(layer_input[0], fwd, sp, dp, width)
    xs = [pieces[0]]
    for r in range(1, sp):
        xs.append(send_sp(pieces[r], r % nx, r // nx))

    q, g = query_states[0], out_grad[0]
    dv_keep, dv_send, lse = probs_call(rel, q, g, kds, sp, tok, win, kvh, group)

    def reduce_core(keep, send):
        return keep + send_sp(send, 0, 1)

    def reduce_all(keep, send):
        here = reduce_core(keep, send)
        total = here
        for k in range(1, nx):
            total = total + jnp.roll(send_sp(here.astype(BF), k, 0), k, axis=0).astype(F32)
        mine = total.astype(BF)
        return mine, send_sp(mine, 0, 1)

    vg0, vg1 = reduce_all(dv_keep, dv_send)

    blocks = wgrad_call(scatter_at, xs, vg0, vg1, sp, nz, ny, tok, width)
    run = None
    for k in range(nz):
        line = blocks[k]
        for j in range(1, ny):
            line = lax.ppermute(line.astype(BF), "dp", y_next).astype(F32) + blocks[nz + k][j - 1]
        line = line.astype(F32)
        run = line if run is None else lax.ppermute(run.astype(BF), "dp", z_next).astype(F32) + line
    weight_grad = run

    v_keep, v_send, w_cols = values_call(gather_at, xs, rows, sp, dp, tok, width)
    v0, v1 = reduce_all(v_keep, v_send)
    dq, dk_keep, dk_send = scores_call(rel, q, g, lse, v0, v1, kds, sp, tok, win, kvh, group)
    dk = reduce_core(dk_keep, dk_send)
    key_sum = dk[0]
    for k in range(1, nx):
        key_sum = key_sum + send_sp(dk[-k % nx].astype(BF), k, 0).astype(F32)
    key_grad = key_sum.astype(BF)

    parts = igrad_call(vg0, vg1, w_cols, sp, tok)
    back = [parts[0]]
    for r in range(1, sp):
        back.append(send_sp(parts[r], -(r % nx), r // nx))
    input_grad = join_columns(back, fwd, sp, dp, width)

    return (dq[None], key_grad[None], input_grad[None], weight_grad)


def solution(mesh):
    in_specs = (
        P("dp", "sp", None),
        P(("dp", "sp"), None),
        P("dp", "sp", None),
        P("dp", "sp", None),
        P("dp", "sp", None),
        P("dp", "sp"),
    )
    out_specs = (
        P("dp", "sp", None),
        P("dp", "sp", None),
        P("dp", "sp", None),
        P(("dp", "sp"), None),
    )
    return jax.shard_map(local, mesh=mesh, in_specs=in_specs, out_specs=out_specs, check_vma=False)
```

```python
import functools
import math

import jax
import jax.numpy as jnp
import numpy as np
from jax import lax
from jax.experimental import pallas as pl
from jax.experimental.pallas import tpu as pltpu
from jax.sharding import PartitionSpec as P

HD = 128
NEG = -1e30
BF = jnp.bfloat16
F32 = jnp.float32
NT = (((1,), (1,)), ((), ()))
TN = (((0,), (0,)), ((), ()))
NN = (((1,), (0,)), ((), ()))
MIB = 1024 * 1024
VM = pl.BlockSpec(memory_space=pltpu.VMEM)
SM = pl.BlockSpec(memory_space=pltpu.SMEM)


def dot(a, b, dims):
    return lax.dot_general(a, b, dims, preferred_element_type=F32)


def ring_order(count):
    return list(range(0, count, 2)) + list(range(1, count, 2))[::-1]


def rows_at(index, size):
    return pl.ds(pl.multiple_of(index * size, size), size)


def grant(mib):
    return pltpu.CompilerParams(vmem_limit_bytes=mib * MIB)


def column_steps(dp, width):
    return max(1, min(4, dp * width // 128 // 2))


def split_kernel(sp, reps, width, base, idx_ref, x_ref, *rest):
    outs, hold = rest[:sp], rest[sp]
    block = reps * width
    at = pl.ds(pl.multiple_of(pl.program_id(0) * block, block), block)
    for a in range(sp):
        for d in range(reps):
            hold[a, :, d * width : (d + 1) * width] = x_ref[
                :, (d * sp + a) * width : (d * sp + a + 1) * width
            ]
    for r in range(sp):
        outs[r][:, at] = hold[idx_ref[base + r]]


def split_columns(idx, base, x, sp, dp, width):
    tok = x.shape[0]
    steps = column_steps(dp, width)
    reps = dp // steps
    block = reps * width
    return pl.pallas_call(
        functools.partial(split_kernel, sp, reps, width, base),
        out_shape=[jax.ShapeDtypeStruct((tok, dp * width), BF)] * sp,
        grid_spec=pltpu.PrefetchScalarGridSpec(
            num_scalar_prefetch=1,
            grid=(steps,),
            in_specs=[pl.BlockSpec((tok, sp * block), lambda d, _: (0, d))],
            out_specs=[VM] * sp,
            scratch_shapes=[pltpu.VMEM((sp, tok, block), BF)],
        ),
        compiler_params=grant(12),
        cost_estimate=pl.CostEstimate(flops=0, bytes_accessed=4 * x.size, transcendentals=0),
        name="split_columns",
    )(idx, x)


def join_kernel(sp, reps, width, base, idx_ref, *rest):
    ins, out, hold = rest[:sp], rest[sp], rest[sp + 1]
    block = reps * width
    at = pl.ds(pl.multiple_of(pl.program_id(0) * block, block), block)
    for r in range(sp):
        hold[idx_ref[base + r]] = ins[r][:, at]
    for a in range(sp):
        for d in range(reps):
            out[:, (d * sp + a) * width : (d * sp + a + 1) * width] = hold[
                a, :, d * width : (d + 1) * width
            ]


def join_columns(idx, base, pieces, sp, dp, width):
    tok = pieces[0].shape[0]
    steps = column_steps(dp, width)
    reps = dp // steps
    block = reps * width
    return pl.pallas_call(
        functools.partial(join_kernel, sp, reps, width, base),
        out_shape=jax.ShapeDtypeStruct((tok, sp * dp * width), BF),
        grid_spec=pltpu.PrefetchScalarGridSpec(
            num_scalar_prefetch=1,
            grid=(steps,),
            in_specs=[VM] * sp,
            out_specs=pl.BlockSpec((tok, sp * block), lambda d, _: (0, d)),
            scratch_shapes=[pltpu.VMEM((sp, tok, block), BF)],
        ),
        compiler_params=grant(12),
        cost_estimate=pl.CostEstimate(
            flops=0, bytes_accessed=4 * tok * sp * dp * width, transcendentals=0
        ),
        name="join_columns",
    )(idx, *pieces)


def fill_keys(sp, tok, win, heads, idx_ref, kd_refs, key_hold, doc_hold, bias):
    first = jnp.maximum(idx_ref[0] + 1 - win, 0)
    head = pl.program_id(0)
    at = pl.ds(pl.multiple_of(head * HD, HD), HD)
    for r in range(sp):
        key_hold[rows_at(idx_ref[r], tok), :] = kd_refs[r][0:tok, at]

    @pl.when(head == 0)
    def _():
        for r in range(sp):
            doc_hold[idx_ref[r]] = kd_refs[r][tok : tok + 16, 0:tok].astype(F32)
        own = jnp.broadcast_to(doc_hold[idx_ref[0]][0:1, :], (tok, tok))
        query_at = idx_ref[0] * tok + lax.broadcasted_iota(jnp.int32, (tok, tok), 1)
        for b in range(win):
            docs = jnp.broadcast_to(doc_hold[first + b][0:1, :], (tok, tok)).T
            key_at = (first + b) * tok + lax.broadcasted_iota(jnp.int32, (tok, tok), 0)
            ok = (key_at <= query_at) & (docs == own)
            block = jnp.where(ok, F32(0.0), F32(NEG))
            for h in range(heads):
                bias[b * tok : (b + 1) * tok, h * tok : (h + 1) * tok] = block

    return first, at


def stack_heads(src, dst, tok, group):
    for h in range(group):
        dst[h * tok : (h + 1) * tok, :] = src[:, h * HD : (h + 1) * HD]


def emit_rel(acc, first, value, sp, tok, win, at, idx_ref, keep, send):
    nx = sp // 2
    acc[...] = jnp.zeros_like(acc)
    acc[pl.ds(pl.multiple_of(first * tok, tok), win * tok), :] = value
    for dx in range(nx):
        keep[dx, :, at] = acc[rows_at(idx_ref[dx], tok), :]
        send[dx, :, at] = acc[rows_at(idx_ref[nx + dx], tok), :]


def probs_kernel(sp, tok, win, group, pair, idx_ref, q_ref, g_ref, *rest):
    kds, (keep, send, lse_ref) = rest[:sp], rest[sp : sp + 3]
    key_hold, doc_hold, bias, q_st, g_st, p_st, acc = rest[sp + 3 :]
    first, cols = fill_keys(sp, tok, win, pair, idx_ref, kds, key_hold, doc_hold, bias)
    factor = F32(HD**-0.5 * math.log2(math.e))
    stack_heads(q_ref, q_st, tok, group)
    stack_heads(g_ref, g_st, tok, group)
    keys = key_hold[pl.ds(pl.multiple_of(first * tok, tok), win * tok), :]
    for h in range(0, group, pair):
        at = slice(h * tok, (h + pair) * tok)
        s = dot(keys, q_st[at, :], NT) * factor + bias[...]
        top = jnp.max(s, axis=0, keepdims=True)
        e = jnp.exp2(s - top)
        total = jnp.sum(e, axis=0, keepdims=True)
        p_st[:, at] = (e * (1.0 / total)).astype(BF)
        lse = top + jnp.log2(total)
        for i in range(pair):
            lse_ref[h + i : h + i + 1, :] = lse[:, i * tok : (i + 1) * tok]
    emit_rel(
        acc, first, dot(p_st[...], g_st[...], NN), sp, tok, win, cols, idx_ref, keep, send
    )


def probs_call(idx, q, g, kds, sp, tok, win, kvh, group):
    nx, seq, pair = sp // 2, sp * tok, 2
    part = jax.ShapeDtypeStruct((nx, tok, kvh * HD), F32)
    wide = pl.BlockSpec((tok, group * HD), lambda c, _: (0, c))
    return pl.pallas_call(
        functools.partial(probs_kernel, sp, tok, win, group, pair),
        out_shape=[part, part, jax.ShapeDtypeStruct((kvh * group, tok), F32)],
        grid_spec=pltpu.PrefetchScalarGridSpec(
            num_scalar_prefetch=1,
            grid=(kvh,),
            in_specs=[wide, wide] + [VM] * sp,
            out_specs=[VM, VM, pl.BlockSpec((group, tok), lambda c, _: (c, 0))],
            scratch_shapes=[
                pltpu.VMEM((seq, HD), BF),
                pltpu.VMEM((sp, 16, tok), F32),
                pltpu.VMEM((win * tok, pair * tok), F32),
                pltpu.VMEM((group * tok, HD), BF),
                pltpu.VMEM((group * tok, HD), BF),
                pltpu.VMEM((win * tok, group * tok), BF),
                pltpu.VMEM((seq, HD), F32),
            ],
        ),
        compiler_params=grant(20),
        cost_estimate=pl.CostEstimate(
            flops=4 * tok * win * tok * kvh * group * HD,
            bytes_accessed=8 * MIB,
            transcendentals=tok * win * tok * kvh * group,
        ),
        name="probs_dv",
    )(idx, q, g, *kds)


def scores_kernel(sp, tok, win, group, pair, idx_ref, q_ref, g_ref, lse_ref, v0_ref, v1_ref, *rest):
    nx = sp // 2
    kds, (dq_ref, keep, send) = rest[:sp], rest[sp : sp + 3]
    key_hold, doc_hold, bias, val_hold, q_st, g_st, ds_st, acc = rest[sp + 3 :]
    first, cols = fill_keys(sp, tok, win, pair, idx_ref, kds, key_hold, doc_hold, bias)
    for dx in range(nx):
        val_hold[rows_at(idx_ref[dx], tok), :] = v0_ref[dx, :, cols]
        val_hold[rows_at(idx_ref[nx + dx], tok), :] = v1_ref[dx, :, cols]
    scale = HD**-0.5
    factor = F32(scale * math.log2(math.e))
    stack_heads(q_ref, q_st, tok, group)
    stack_heads(g_ref, g_st, tok, group)
    window = pl.ds(pl.multiple_of(first * tok, tok), win * tok)
    keys, vals = key_hold[window, :], val_hold[window, :]
    for h in range(0, group, pair):
        at = slice(h * tok, (h + pair) * tok)
        lse = jnp.concatenate([lse_ref[h + i : h + i + 1, :] for i in range(pair)], axis=1)
        shift = lse - F32(math.log2(scale))
        s = dot(keys, q_st[at, :], NT) * factor + bias[...]
        scaled = jnp.exp2(s - shift)
        dp = dot(vals, g_st[at, :], NT)
        delta = jnp.sum(scaled * dp, axis=0, keepdims=True) * F32(1.0 / scale)
        ds_st[:, at] = (scaled * (dp - delta)).astype(BF)
    dq = dot(ds_st[...], keys, TN)
    for h in range(group):
        dq_ref[:, h * HD : (h + 1) * HD] = dq[h * tok : (h + 1) * tok, :].astype(BF)
    emit_rel(
        acc, first, dot(ds_st[...], q_st[...], NN), sp, tok, win, cols, idx_ref, keep, send
    )


def scores_call(idx, q, g, lse, v0, v1, kds, sp, tok, win, kvh, group):
    nx, seq, pair = sp // 2, sp * tok, 2
    part = jax.ShapeDtypeStruct((nx, tok, kvh * HD), F32)
    wide = pl.BlockSpec((tok, group * HD), lambda c, _: (0, c))
    return pl.pallas_call(
        functools.partial(scores_kernel, sp, tok, win, group, pair),
        out_shape=[jax.ShapeDtypeStruct(q.shape, BF), part, part],
        grid_spec=pltpu.PrefetchScalarGridSpec(
            num_scalar_prefetch=1,
            grid=(kvh,),
            in_specs=[wide, wide, pl.BlockSpec((group, tok), lambda c, _: (c, 0)), VM, VM]
            + [VM] * sp,
            out_specs=[wide, VM, VM],
            scratch_shapes=[
                pltpu.VMEM((seq, HD), BF),
                pltpu.VMEM((sp, 16, tok), F32),
                pltpu.VMEM((win * tok, pair * tok), F32),
                pltpu.VMEM((seq, HD), BF),
                pltpu.VMEM((group * tok, HD), BF),
                pltpu.VMEM((group * tok, HD), BF),
                pltpu.VMEM((win * tok, group * tok), BF),
                pltpu.VMEM((seq, HD), F32),
            ],
        ),
        compiler_params=grant(24),
        cost_estimate=pl.CostEstimate(
            flops=8 * tok * win * tok * kvh * group * HD,
            bytes_accessed=10 * MIB,
            transcendentals=tok * win * tok * kvh * group,
        ),
        name="scores_dq_dk",
    )(idx, q, g, lse, v0, v1, *kds)


def values_kernel(sp, dp, tok, width, base, idx_ref, *rest):
    nx = sp // 2
    xs, ws = rest[:sp], rest[sp : sp + dp]
    keep, send, x_hold, w_hold = rest[sp + dp :]
    for i in range(dp):
        w_hold[rows_at(idx_ref[base + i], width), :] = ws[i][...]
    for r in range(sp):
        x_hold[r * tok : (r + 1) * tok, :] = xs[r][...]
    out = dot(x_hold[...], w_hold[...], NN)
    for dx in range(nx):
        keep[dx] = out[dx * tok : (dx + 1) * tok]
        send[dx] = out[(nx + dx) * tok : (nx + dx + 1) * tok]


def values_call(idx, base, xs, ws, sp, dp, tok, width):
    nx, kv = sp // 2, ws[0].shape[1]
    cols = dp * width
    part = jax.ShapeDtypeStruct((nx, tok, kv), F32)
    return pl.pallas_call(
        functools.partial(values_kernel, sp, dp, tok, width, base),
        out_shape=[part, part],
        in_specs=[SM] + [VM] * (sp + dp),
        out_specs=[VM] * 2,
        scratch_shapes=[pltpu.VMEM((sp * tok, cols), BF), pltpu.VMEM((cols, kv), BF)],
        compiler_params=grant(16),
        cost_estimate=pl.CostEstimate(
            flops=2 * sp * tok * cols * kv, bytes_accessed=8 * MIB, transcendentals=0
        ),
        name="values_part",
    )(idx, *xs, *ws)


def wgrad_kernel(sp, nz, ny, tok, width, base, idx_ref, *rest):
    nx = sp // 2
    xs, (g0, g1) = rest[:sp], rest[sp : sp + 2]
    outs = rest[sp + 2 : sp + 2 + 2 * nz]
    x_hold, g_hold, total = rest[sp + 2 + 2 * nz :]
    for dx in range(nx):
        for core, src in ((0, g0), (1, g1)):
            r = core * nx + dx
            x_hold[r * tok : (r + 1) * tok, :] = xs[r][...]
            g_hold[r * tok : (r + 1) * tok, :] = src[dx]
    cols = x_hold.shape[1]
    step = min(cols, 512)
    for at in range(0, cols, step):
        total[at : at + step, :] = dot(x_hold[:, at : at + step], g_hold[...], TN)
    for k in range(nz):
        outs[k][...] = total[rows_at(idx_ref[base + k * ny], width), :].astype(BF)
        for j in range(1, ny):
            outs[nz + k][j - 1] = total[rows_at(idx_ref[base + k * ny + j], width), :]


def wgrad_call(idx, base, xs, g0, g1, sp, nz, ny, tok, width):
    nx, kv = sp // 2, g0.shape[2]
    cols = nz * ny * width
    return pl.pallas_call(
        functools.partial(wgrad_kernel, sp, nz, ny, tok, width, base),
        out_shape=[jax.ShapeDtypeStruct((width, kv), BF)] * nz
        + [jax.ShapeDtypeStruct((ny - 1, width, kv), F32)] * nz,
        in_specs=[SM] + [VM] * (sp + 2),
        out_specs=[VM] * (2 * nz),
        scratch_shapes=[
            pltpu.VMEM((sp * tok, cols), BF),
            pltpu.VMEM((sp * tok, kv), BF),
            pltpu.VMEM((cols, kv), F32),
        ],
        compiler_params=grant(20),
        cost_estimate=pl.CostEstimate(
            flops=2 * sp * tok * cols * kv, bytes_accessed=7 * MIB, transcendentals=0
        ),
        name="weight_grad_part",
    )(idx, *xs, g0, g1)


def igrad_kernel(sp, dp, tok, width, base, idx_ref, g0, g1, *rest):
    nx = sp // 2
    ws, outs = rest[:dp], rest[dp : dp + sp]
    g_hold, w_hold = rest[dp + sp :]
    for i in range(dp):
        w_hold[rows_at(idx_ref[base + i], width), :] = ws[i][...]
    for dx in range(nx):
        g_hold[dx * tok : (dx + 1) * tok, :] = g0[dx]
        g_hold[(nx + dx) * tok : (nx + dx + 1) * tok, :] = g1[dx]
    cols = w_hold.shape[0]
    step = min(cols, 512)
    for at in range(0, cols, step):
        out = dot(g_hold[...], w_hold[at : at + step, :], NT)
        for r in range(sp):
            outs[r][:, at : at + step] = out[r * tok : (r + 1) * tok].astype(BF)


def igrad_call(idx, base, g0, g1, ws, sp, dp, tok, width):
    kv = g0.shape[2]
    cols = dp * width
    return pl.pallas_call(
        functools.partial(igrad_kernel, sp, dp, tok, width, base),
        out_shape=[jax.ShapeDtypeStruct((tok, cols), BF)] * sp,
        in_specs=[SM] + [VM] * (2 + dp),
        out_specs=[VM] * sp,
        scratch_shapes=[pltpu.VMEM((sp * tok, kv), BF), pltpu.VMEM((cols, kv), BF)],
        compiler_params=grant(16),
        cost_estimate=pl.CostEstimate(
            flops=2 * sp * tok * cols * kv, bytes_accessed=5 * MIB, transcendentals=0
        ),
        name="input_grad_part",
    )(idx, g0, g1, *ws)


def after(value, *others):
    return lax.optimization_barrier((value, *others))[0]


def local(layer_input, value_weight, query_states, key_states, out_grad, doc_ids):
    sp, dp = lax.axis_size("sp"), lax.axis_size("dp")
    nx = sp // 2
    ny = max(1, min(nx, dp))
    nz = dp // ny
    tok = layer_input.shape[1]
    width = value_weight.shape[0]
    kvh = key_states.shape[2] // HD
    group = query_states.shape[2] // HD // kvh
    win = min(sp, sp // 2 + 1)

    def sp_perm(dx, dc):
        return [(i, ((i // 2 + dx) % nx) * 2 + (i % 2 ^ dc)) for i in range(sp)]

    def send_sp(v, dx, dc):
        return lax.ppermute(v, "sp", sp_perm(dx % nx, dc))

    z_ring, y_ring = ring_order(nz), ring_order(ny)

    def pred(ring, at, k):
        return ring[(ring.index(at) - k) % len(ring)]

    z_next = [
        (z_ring[p] * ny + y, z_ring[(p + 1) % nz] * ny + y) for p in range(nz) for y in range(ny)
    ]
    y_next = [
        (z * ny + y_ring[p], z * ny + y_ring[(p + 1) % ny]) for p in range(ny) for z in range(nz)
    ]

    def send_z(v):
        return lax.ppermute(v, "dp", z_next)

    def send_y(v):
        return lax.ppermute(v, "dp", y_next)

    table = []
    for d in range(dp):
        z, y = d // ny, d % ny
        for s in range(sp):
            x, core = s // 2, s % 2
            row = [((x - dx) % nx) * 2 + (core ^ dc) for dc in range(2) for dx in range(nx)]
            row += [((x + dx) % nx) * 2 + (core ^ dc) for dc in range(2) for dx in range(nx)]
            row += [pred(z_ring, z, k) * ny + pred(y_ring, y, j) for k in range(nz) for j in range(ny)]
            row += [
                pred(z_ring, z, k) * ny + pred(y_ring, y, j)
                for k in range(1, nz + 1)
                for j in range(1, ny + 1)
            ]
            table.append(row)
    at_fwd, at_gather, at_scatter = sp, 2 * sp, 2 * sp + dp
    flat = lax.axis_index("dp") * sp + lax.axis_index("sp")
    idx = lax.dynamic_index_in_dim(jnp.asarray(table, jnp.int32), flat, 0, keepdims=False)

    q, g = query_states[0], out_grad[0]

    doc_rows = jnp.pad(
        jnp.broadcast_to(doc_ids.astype(BF), (16, tok)), ((0, 0), (0, kvh * HD - tok))
    )
    kd = jnp.concatenate([key_states[0], doc_rows], axis=0)
    near = [kd] + [send_sp(kd, dx, 0) for dx in range(1, nx)]
    kds = near + [send_sp(v, 0, 1) for v in near]

    z_rows = [value_weight]
    for k in range(1, nz):
        z_rows.append(send_z(z_rows[-1]))
    rows = []
    for v in z_rows:
        for j in range(ny):
            rows.append(v)
            if j + 1 < ny:
                v = send_y(v)

    pieces = split_columns(idx, at_fwd, layer_input[0], sp, dp, width)
    ready = [pieces[0]] + [after(v, near[-1]) for v in pieces[1:]]

    kds = list(lax.optimization_barrier((*kds, *ready[1:], z_rows[min(1, nz - 1)]))[:sp])
    dv_keep, dv_send, lse = probs_call(idx, q, g, kds, sp, tok, win, kvh, group)

    def reduce_core(keep, send):
        return keep + send_sp(send, 0, 1)

    def reduce_all(keep, send):
        here = reduce_core(keep, send)
        small = here.astype(BF)
        total, got = here, small
        for k in range(1, nx):
            got = send_sp(small, k, 0)
            total = total + jnp.roll(got, k, axis=0).astype(F32)
        mine = total.astype(BF)
        return mine, send_sp(mine, 0, 1), got

    vg0, vg1, vg_got = reduce_all(dv_keep, dv_send)

    xs = [pieces[0]]
    for r in range(1, sp):
        dx, dc = r % nx, r // nx
        v = after(ready[r], vg_got) if dx and dc else ready[r]
        xs.append(send_sp(v, dx, dc))

    parts = igrad_call(idx, at_gather, vg0, vg1, rows, sp, dp, tok, width)

    blocks = wgrad_call(idx, at_scatter, xs, vg0, vg1, sp, nz, ny, tok, width)
    run = None
    for k in range(nz):
        line = blocks[k]
        for j in range(1, ny):
            line = send_y(line.astype(BF)).astype(F32) + blocks[nz + k][j - 1]
        line = line.astype(F32)
        run = line if run is None else send_z(run.astype(BF)).astype(F32) + line
    weight_grad = run

    v_keep, v_send = values_call(idx, at_gather, xs, rows, sp, dp, tok, width)
    v0, v1, v_got = reduce_all(v_keep, v_send)
    dq, dk_keep, dk_send = scores_call(idx, q, g, lse, v0, v1, kds, sp, tok, win, kvh, group)
    dk = reduce_core(dk_keep, dk_send)
    key_sum = dk[0]
    for k in range(1, nx):
        key_sum = key_sum + send_sp(dk[-k % nx].astype(BF), k, 0).astype(F32)
    key_grad = key_sum.astype(BF)

    back = [parts[0]]
    for r in range(1, sp):
        dx, dc = r % nx, r // nx
        v = after(parts[r], v_got) if dx and dc else parts[r]
        back.append(send_sp(v, -dx, dc))
    input_grad = join_columns(idx, at_fwd, back, sp, dp, width)

    return (dq[None], key_grad[None], input_grad[None], weight_grad)


def solution(mesh):
    in_specs = (
        P("dp", "sp", None),
        P(("dp", "sp"), None),
        P("dp", "sp", None),
        P("dp", "sp", None),
        P("dp", "sp", None),
        P("dp", "sp"),
    )
    out_specs = (
        P("dp", "sp", None),
        P("dp", "sp", None),
        P("dp", "sp", None),
        P(("dp", "sp"), None),
    )
    return jax.shard_map(local, mesh=mesh, in_specs=in_specs, out_specs=out_specs, check_vma=False)
```

```python
import functools
import math

import jax
import jax.numpy as jnp
from jax import lax
from jax.experimental import pallas as pl
from jax.experimental.pallas import tpu as pltpu
from jax.sharding import PartitionSpec as P

HD = 128
NEG = -1e30
BF = jnp.bfloat16
F32 = jnp.float32
NT = (((1,), (1,)), ((), ()))
TN = (((0,), (0,)), ((), ()))
NN = (((1,), (0,)), ((), ()))
MIB = 1024 * 1024
VM = pl.BlockSpec(memory_space=pltpu.VMEM)
SM = pl.BlockSpec(memory_space=pltpu.SMEM)


def dot(a, b, dims):
    return lax.dot_general(a, b, dims, preferred_element_type=F32)


def ring_order(count):
    return list(range(0, count, 2)) + list(range(1, count, 2))[::-1]


def rows_at(index, size):
    return pl.ds(pl.multiple_of(index * size, size), size)


def grant(mib):
    return pltpu.CompilerParams(vmem_limit_bytes=mib * MIB)


def column_steps(dp, width):
    return max(1, min(4, dp * width // 128 // 2))


def split_kernel(sp, reps, width, base, idx_ref, x_ref, *rest):
    outs, hold = rest[:sp], rest[sp]
    block = reps * width
    at = pl.ds(pl.multiple_of(pl.program_id(0) * block, block), block)
    for a in range(sp):
        for d in range(reps):
            hold[a, :, d * width : (d + 1) * width] = x_ref[
                :, (d * sp + a) * width : (d * sp + a + 1) * width
            ]
    for r in range(sp):
        outs[r][:, at] = hold[idx_ref[base + r]]


def split_columns(idx, base, x, sp, dp, width):
    tok = x.shape[0]
    steps = column_steps(dp, width)
    reps = dp // steps
    block = reps * width
    return pl.pallas_call(
        functools.partial(split_kernel, sp, reps, width, base),
        out_shape=[jax.ShapeDtypeStruct((tok, dp * width), BF)] * sp,
        grid_spec=pltpu.PrefetchScalarGridSpec(
            num_scalar_prefetch=1,
            grid=(steps,),
            in_specs=[pl.BlockSpec((tok, sp * block), lambda d, _: (0, d))],
            out_specs=[VM] * sp,
            scratch_shapes=[pltpu.VMEM((sp, tok, block), BF)],
        ),
        compiler_params=grant(12),
        cost_estimate=pl.CostEstimate(flops=0, bytes_accessed=4 * x.size, transcendentals=0),
        name="split_columns",
    )(idx, x)


def join_kernel(sp, reps, width, base, idx_ref, *rest):
    ins, out, hold = rest[:sp], rest[sp], rest[sp + 1]
    block = reps * width
    at = pl.ds(pl.multiple_of(pl.program_id(0) * block, block), block)
    for r in range(sp):
        hold[idx_ref[base + r]] = ins[r][:, at]
    for a in range(sp):
        for d in range(reps):
            out[:, (d * sp + a) * width : (d * sp + a + 1) * width] = hold[
                a, :, d * width : (d + 1) * width
            ]


def join_columns(idx, base, pieces, sp, dp, width):
    tok = pieces[0].shape[0]
    steps = column_steps(dp, width)
    reps = dp // steps
    block = reps * width
    return pl.pallas_call(
        functools.partial(join_kernel, sp, reps, width, base),
        out_shape=jax.ShapeDtypeStruct((tok, sp * dp * width), BF),
        grid_spec=pltpu.PrefetchScalarGridSpec(
            num_scalar_prefetch=1,
            grid=(steps,),
            in_specs=[VM] * sp,
            out_specs=pl.BlockSpec((tok, sp * block), lambda d, _: (0, d)),
            scratch_shapes=[pltpu.VMEM((sp, tok, block), BF)],
        ),
        compiler_params=grant(12),
        cost_estimate=pl.CostEstimate(
            flops=0, bytes_accessed=4 * tok * sp * dp * width, transcendentals=0
        ),
        name="join_columns",
    )(idx, *pieces)


def fill_keys(sp, tok, win, heads, idx_ref, kd_refs, key_hold, doc_hold, bias):
    first = jnp.maximum(idx_ref[0] + 1 - win, 0)
    head = pl.program_id(0)
    at = pl.ds(pl.multiple_of(head * HD, HD), HD)
    for r in range(sp):
        key_hold[rows_at(idx_ref[r], tok), :] = kd_refs[r][0:tok, at]

    @pl.when(head == 0)
    def _():
        for r in range(sp):
            doc_hold[idx_ref[r]] = kd_refs[r][tok : tok + 16, 0:tok].astype(F32)
        own = jnp.broadcast_to(doc_hold[idx_ref[0]][0:1, :], (tok, tok))
        query_at = idx_ref[0] * tok + lax.broadcasted_iota(jnp.int32, (tok, tok), 1)
        for b in range(win):
            docs = jnp.broadcast_to(doc_hold[first + b][0:1, :], (tok, tok)).T
            key_at = (first + b) * tok + lax.broadcasted_iota(jnp.int32, (tok, tok), 0)
            ok = (key_at <= query_at) & (docs == own)
            block = jnp.where(ok, F32(0.0), F32(NEG))
            for h in range(heads):
                bias[b * tok : (b + 1) * tok, h * tok : (h + 1) * tok] = block

    return first, at


def stack_heads(src, dst, tok, group):
    for h in range(group):
        dst[h * tok : (h + 1) * tok, :] = src[:, h * HD : (h + 1) * HD]


def emit_rel(acc, first, value, sp, tok, win, at, idx_ref, keep, send):
    nx = sp // 2
    acc[...] = jnp.zeros_like(acc)
    acc[pl.ds(pl.multiple_of(first * tok, tok), win * tok), :] = value
    for dx in range(nx):
        keep[dx, :, at] = acc[rows_at(idx_ref[dx], tok), :]
        send[dx, :, at] = acc[rows_at(idx_ref[nx + dx], tok), :]


def probs_kernel(sp, tok, win, group, pair, idx_ref, q_ref, g_ref, *rest):
    kds, (keep, send, lse_ref) = rest[:sp], rest[sp : sp + 3]
    key_hold, doc_hold, bias, q_st, g_st, p_st, acc = rest[sp + 3 :]
    first, cols = fill_keys(sp, tok, win, pair, idx_ref, kds, key_hold, doc_hold, bias)
    factor = F32(HD**-0.5 * math.log2(math.e))
    stack_heads(q_ref, q_st, tok, group)
    stack_heads(g_ref, g_st, tok, group)
    keys = key_hold[pl.ds(pl.multiple_of(first * tok, tok), win * tok), :]
    for h in range(0, group, pair):
        at = slice(h * tok, (h + pair) * tok)
        s = dot(keys, q_st[at, :], NT) * factor + bias[...]
        top = jnp.max(s, axis=0, keepdims=True)
        e = jnp.exp2(s - top)
        total = jnp.sum(e, axis=0, keepdims=True)
        p_st[:, at] = (e * (1.0 / total)).astype(BF)
        lse = top + jnp.log2(total)
        for i in range(pair):
            lse_ref[h + i : h + i + 1, :] = lse[:, i * tok : (i + 1) * tok]
    emit_rel(
        acc, first, dot(p_st[...], g_st[...], NN), sp, tok, win, cols, idx_ref, keep, send
    )


def probs_call(idx, q, g, kds, sp, tok, win, kvh, group):
    nx, seq, pair = sp // 2, sp * tok, 2
    part = jax.ShapeDtypeStruct((nx, tok, kvh * HD), F32)
    wide = pl.BlockSpec((tok, group * HD), lambda c, _: (0, c))
    return pl.pallas_call(
        functools.partial(probs_kernel, sp, tok, win, group, pair),
        out_shape=[part, part, jax.ShapeDtypeStruct((kvh * group, tok), F32)],
        grid_spec=pltpu.PrefetchScalarGridSpec(
            num_scalar_prefetch=1,
            grid=(kvh,),
            in_specs=[wide, wide] + [VM] * sp,
            out_specs=[VM, VM, pl.BlockSpec((group, tok), lambda c, _: (c, 0))],
            scratch_shapes=[
                pltpu.VMEM((seq, HD), BF),
                pltpu.VMEM((sp, 16, tok), F32),
                pltpu.VMEM((win * tok, pair * tok), F32),
                pltpu.VMEM((group * tok, HD), BF),
                pltpu.VMEM((group * tok, HD), BF),
                pltpu.VMEM((win * tok, group * tok), BF),
                pltpu.VMEM((seq, HD), F32),
            ],
        ),
        compiler_params=grant(20),
        cost_estimate=pl.CostEstimate(
            flops=4 * tok * win * tok * kvh * group * HD,
            bytes_accessed=8 * MIB,
            transcendentals=tok * win * tok * kvh * group,
        ),
        name="probs_dv",
    )(idx, q, g, *kds)


def scores_kernel(sp, tok, win, group, pair, idx_ref, q_ref, g_ref, lse_ref, v0_ref, v1_ref, *rest):
    nx = sp // 2
    kds, (dq_ref, keep, send) = rest[:sp], rest[sp : sp + 3]
    key_hold, doc_hold, bias, val_hold, q_st, g_st, ds_st, acc = rest[sp + 3 :]
    first, cols = fill_keys(sp, tok, win, pair, idx_ref, kds, key_hold, doc_hold, bias)
    for dx in range(nx):
        val_hold[rows_at(idx_ref[dx], tok), :] = v0_ref[dx, :, cols]
        val_hold[rows_at(idx_ref[nx + dx], tok), :] = v1_ref[dx, :, cols]
    scale = HD**-0.5
    factor = F32(scale * math.log2(math.e))
    stack_heads(q_ref, q_st, tok, group)
    stack_heads(g_ref, g_st, tok, group)
    window = pl.ds(pl.multiple_of(first * tok, tok), win * tok)
    keys, vals = key_hold[window, :], val_hold[window, :]
    for h in range(0, group, pair):
        at = slice(h * tok, (h + pair) * tok)
        lse = jnp.concatenate([lse_ref[h + i : h + i + 1, :] for i in range(pair)], axis=1)
        shift = lse - F32(math.log2(scale))
        s = dot(keys, q_st[at, :], NT) * factor + bias[...]
        scaled = jnp.exp2(s - shift)
        dp = dot(vals, g_st[at, :], NT)
        delta = jnp.sum(scaled * dp, axis=0, keepdims=True) * F32(1.0 / scale)
        ds_st[:, at] = (scaled * (dp - delta)).astype(BF)
    dq = dot(ds_st[...], keys, TN)
    for h in range(group):
        dq_ref[:, h * HD : (h + 1) * HD] = dq[h * tok : (h + 1) * tok, :].astype(BF)
    emit_rel(
        acc, first, dot(ds_st[...], q_st[...], NN), sp, tok, win, cols, idx_ref, keep, send
    )


def scores_call(idx, q, g, lse, v0, v1, kds, sp, tok, win, kvh, group):
    nx, seq, pair = sp // 2, sp * tok, 2
    part = jax.ShapeDtypeStruct((nx, tok, kvh * HD), F32)
    wide = pl.BlockSpec((tok, group * HD), lambda c, _: (0, c))
    return pl.pallas_call(
        functools.partial(scores_kernel, sp, tok, win, group, pair),
        out_shape=[jax.ShapeDtypeStruct(q.shape, BF), part, part],
        grid_spec=pltpu.PrefetchScalarGridSpec(
            num_scalar_prefetch=1,
            grid=(kvh,),
            in_specs=[wide, wide, pl.BlockSpec((group, tok), lambda c, _: (c, 0)), VM, VM]
            + [VM] * sp,
            out_specs=[wide, VM, VM],
            scratch_shapes=[
                pltpu.VMEM((seq, HD), BF),
                pltpu.VMEM((sp, 16, tok), F32),
                pltpu.VMEM((win * tok, pair * tok), F32),
                pltpu.VMEM((seq, HD), BF),
                pltpu.VMEM((group * tok, HD), BF),
                pltpu.VMEM((group * tok, HD), BF),
                pltpu.VMEM((win * tok, group * tok), BF),
                pltpu.VMEM((seq, HD), F32),
            ],
        ),
        compiler_params=grant(24),
        cost_estimate=pl.CostEstimate(
            flops=8 * tok * win * tok * kvh * group * HD,
            bytes_accessed=10 * MIB,
            transcendentals=tok * win * tok * kvh * group,
        ),
        name="scores_dq_dk",
    )(idx, q, g, lse, v0, v1, *kds)


def values_kernel(sp, dp, tok, width, base, idx_ref, *rest):
    nx = sp // 2
    xs, ws = rest[:sp], rest[sp : sp + dp]
    keep, send, x_hold, w_hold = rest[sp + dp :]
    for i in range(dp):
        w_hold[rows_at(idx_ref[base + i], width), :] = ws[i][...]
    for r in range(sp):
        x_hold[r * tok : (r + 1) * tok, :] = xs[r][...]
    out = dot(x_hold[...], w_hold[...], NN)
    for dx in range(nx):
        keep[dx] = out[dx * tok : (dx + 1) * tok]
        send[dx] = out[(nx + dx) * tok : (nx + dx + 1) * tok]


def values_call(idx, base, xs, ws, sp, dp, tok, width):
    nx, kv = sp // 2, ws[0].shape[1]
    cols = dp * width
    part = jax.ShapeDtypeStruct((nx, tok, kv), F32)
    return pl.pallas_call(
        functools.partial(values_kernel, sp, dp, tok, width, base),
        out_shape=[part, part],
        in_specs=[SM] + [VM] * (sp + dp),
        out_specs=[VM] * 2,
        scratch_shapes=[pltpu.VMEM((sp * tok, cols), BF), pltpu.VMEM((cols, kv), BF)],
        compiler_params=grant(16),
        cost_estimate=pl.CostEstimate(
            flops=2 * sp * tok * cols * kv, bytes_accessed=8 * MIB, transcendentals=0
        ),
        name="values_part",
    )(idx, *xs, *ws)


def wgrad_kernel(sp, nz, ny, tok, width, base, idx_ref, *rest):
    nx = sp // 2
    xs, (g0, g1) = rest[:sp], rest[sp : sp + 2]
    outs = rest[sp + 2 : sp + 2 + 2 * nz]
    x_hold, g_hold, total = rest[sp + 2 + 2 * nz :]
    for dx in range(nx):
        for core, src in ((0, g0), (1, g1)):
            r = core * nx + dx
            x_hold[r * tok : (r + 1) * tok, :] = xs[r][...]
            g_hold[r * tok : (r + 1) * tok, :] = src[dx]
    cols = x_hold.shape[1]
    step = min(cols, 512)
    for at in range(0, cols, step):
        total[at : at + step, :] = dot(x_hold[:, at : at + step], g_hold[...], TN)
    for k in range(nz):
        outs[k][...] = total[rows_at(idx_ref[base + k * ny], width), :].astype(BF)
        for j in range(1, ny):
            outs[nz + k][j - 1] = total[rows_at(idx_ref[base + k * ny + j], width), :]


def wgrad_call(idx, base, xs, g0, g1, sp, nz, ny, tok, width):
    kv = g0.shape[2]
    cols = nz * ny * width
    return pl.pallas_call(
        functools.partial(wgrad_kernel, sp, nz, ny, tok, width, base),
        out_shape=[jax.ShapeDtypeStruct((width, kv), BF)] * nz
        + [jax.ShapeDtypeStruct((ny - 1, width, kv), F32)] * nz,
        in_specs=[SM] + [VM] * (sp + 2),
        out_specs=[VM] * (2 * nz),
        scratch_shapes=[
            pltpu.VMEM((sp * tok, cols), BF),
            pltpu.VMEM((sp * tok, kv), BF),
            pltpu.VMEM((cols, kv), F32),
        ],
        compiler_params=grant(20),
        cost_estimate=pl.CostEstimate(
            flops=2 * sp * tok * cols * kv, bytes_accessed=7 * MIB, transcendentals=0
        ),
        name="weight_grad_part",
    )(idx, *xs, g0, g1)


def igrad_kernel(sp, dp, tok, width, base, idx_ref, g0, g1, *rest):
    nx = sp // 2
    ws, outs = rest[:dp], rest[dp : dp + sp]
    g_hold, w_hold = rest[dp + sp :]
    for i in range(dp):
        w_hold[rows_at(idx_ref[base + i], width), :] = ws[i][...]
    for dx in range(nx):
        g_hold[dx * tok : (dx + 1) * tok, :] = g0[dx]
        g_hold[(nx + dx) * tok : (nx + dx + 1) * tok, :] = g1[dx]
    cols = w_hold.shape[0]
    step = min(cols, 512)
    for at in range(0, cols, step):
        out = dot(g_hold[...], w_hold[at : at + step, :], NT)
        for r in range(sp):
            outs[r][:, at : at + step] = out[r * tok : (r + 1) * tok].astype(BF)


def igrad_call(idx, base, g0, g1, ws, sp, dp, tok, width):
    kv = g0.shape[2]
    cols = dp * width
    return pl.pallas_call(
        functools.partial(igrad_kernel, sp, dp, tok, width, base),
        out_shape=[jax.ShapeDtypeStruct((tok, cols), BF)] * sp,
        in_specs=[SM] + [VM] * (2 + dp),
        out_specs=[VM] * sp,
        scratch_shapes=[pltpu.VMEM((sp * tok, kv), BF), pltpu.VMEM((cols, kv), BF)],
        compiler_params=grant(16),
        cost_estimate=pl.CostEstimate(
            flops=2 * sp * tok * cols * kv, bytes_accessed=5 * MIB, transcendentals=0
        ),
        name="input_grad_part",
    )(idx, g0, g1, *ws)


def after(value, *others):
    return lax.optimization_barrier((value, *others))[0]


def local(layer_input, value_weight, query_states, key_states, out_grad, doc_ids):
    sp, dp = lax.axis_size("sp"), lax.axis_size("dp")
    nx = sp // 2
    ny = max(1, min(nx, dp))
    nz = dp // ny
    tok = layer_input.shape[1]
    width = value_weight.shape[0]
    kvh = key_states.shape[2] // HD
    group = query_states.shape[2] // HD // kvh
    win = min(sp, sp // 2 + 1)

    def sp_perm(dx, dc):
        return [(i, ((i // 2 + dx) % nx) * 2 + (i % 2 ^ dc)) for i in range(sp)]

    def send_sp(v, dx, dc):
        return lax.ppermute(v, "sp", sp_perm(dx % nx, dc))

    z_ring, y_ring = ring_order(nz), ring_order(ny)

    def pred(ring, at, k):
        return ring[(ring.index(at) - k) % len(ring)]

    z_next = [
        (z_ring[p] * ny + y, z_ring[(p + 1) % nz] * ny + y) for p in range(nz) for y in range(ny)
    ]
    y_next = [
        (z * ny + y_ring[p], z * ny + y_ring[(p + 1) % ny]) for p in range(ny) for z in range(nz)
    ]

    def send_z(v):
        return lax.ppermute(v, "dp", z_next)

    def send_y(v):
        return lax.ppermute(v, "dp", y_next)

    table = []
    for d in range(dp):
        z, y = d // ny, d % ny
        for s in range(sp):
            x, core = s // 2, s % 2
            row = [((x - dx) % nx) * 2 + (core ^ dc) for dc in range(2) for dx in range(nx)]
            row += [((x + dx) % nx) * 2 + (core ^ dc) for dc in range(2) for dx in range(nx)]
            row += [pred(z_ring, z, k) * ny + pred(y_ring, y, j) for k in range(nz) for j in range(ny)]
            row += [
                pred(z_ring, z, k) * ny + pred(y_ring, y, j)
                for k in range(1, nz + 1)
                for j in range(1, ny + 1)
            ]
            table.append(row)
    at_fwd, at_gather, at_scatter = sp, 2 * sp, 2 * sp + dp
    flat = lax.axis_index("dp") * sp + lax.axis_index("sp")
    idx = lax.dynamic_index_in_dim(jnp.asarray(table, jnp.int32), flat, 0, keepdims=False)

    q, g = query_states[0], out_grad[0]

    doc_rows = jnp.pad(
        jnp.broadcast_to(doc_ids.astype(BF), (16, tok)), ((0, 0), (0, kvh * HD - tok))
    )
    kd = jnp.concatenate([key_states[0], doc_rows], axis=0)
    near = [kd] + [send_sp(kd, dx, 0) for dx in range(1, nx)]
    kds = near + [send_sp(v, 0, 1) for v in near]

    z_rows = [value_weight]
    for _ in range(1, nz):
        z_rows.append(send_z(z_rows[-1]))
    rows = []
    for v in z_rows:
        for j in range(ny):
            rows.append(v)
            if j + 1 < ny:
                v = send_y(v)

    pieces = split_columns(idx, at_fwd, layer_input[0], sp, dp, width)
    ready = [pieces[0]] + [after(v, near[-1]) for v in pieces[1:]]

    kds = list(lax.optimization_barrier((*kds, z_rows[min(1, nz - 1)]))[:sp])
    dv_keep, dv_send, lse = probs_call(idx, q, g, kds, sp, tok, win, kvh, group)

    def reduce_core(keep, send):
        return keep + send_sp(send, 0, 1)

    def reduce_all(keep, send):
        here = reduce_core(keep, send)
        small = here.astype(BF)
        total, got = here, small
        for k in range(1, nx):
            got = send_sp(small, k, 0)
            total = total + jnp.roll(got, k, axis=0).astype(F32)
        mine = total.astype(BF)
        return mine, send_sp(mine, 0, 1), got

    vg0, vg1, vg_got = reduce_all(dv_keep, dv_send)

    xs = [pieces[0]]
    for r in range(1, sp):
        dx, dc = r % nx, r // nx
        if dx and dc:
            xs.append(send_sp(after(ready[r], vg_got), dx, dc))
        else:
            xs.append(send_sp(ready[r], dx, dc))

    parts = igrad_call(idx, at_gather, vg0, vg1, rows, sp, dp, tok, width)

    blocks = wgrad_call(idx, at_scatter, xs, vg0, vg1, sp, nz, ny, tok, width)
    run = None
    for k in range(nz):
        line = blocks[k]
        for j in range(1, ny):
            line = send_y(line.astype(BF)).astype(F32) + blocks[nz + k][j - 1]
        line = line.astype(F32)
        run = line if run is None else send_z(run.astype(BF)).astype(F32) + line
    weight_grad = run

    v_keep, v_send = values_call(idx, at_gather, xs, rows, sp, dp, tok, width)
    v0, v1, v_got = reduce_all(v_keep, v_send)
    dq, dk_keep, dk_send = scores_call(idx, q, g, lse, v0, v1, kds, sp, tok, win, kvh, group)
    dk = reduce_core(dk_keep, dk_send)
    key_sum = dk[0]
    for k in range(1, nx):
        key_sum = key_sum + send_sp(dk[-k % nx].astype(BF), k, 0).astype(F32)
    key_grad = key_sum.astype(BF)

    back = [parts[0]]
    for r in range(1, sp):
        dx, dc = r % nx, r // nx
        if dx and dc:
            back.append(send_sp(after(parts[r], v_got), -dx, dc))
        else:
            back.append(send_sp(parts[r], -dx, dc))
    input_grad = join_columns(idx, at_fwd, back, sp, dp, width)

    return (dq[None], key_grad[None], input_grad[None], weight_grad)


def solution(mesh):
    in_specs = (
        P("dp", "sp", None),
        P(("dp", "sp"), None),
        P("dp", "sp", None),
        P("dp", "sp", None),
        P("dp", "sp", None),
        P("dp", "sp"),
    )
    out_specs = (
        P("dp", "sp", None),
        P("dp", "sp", None),
        P("dp", "sp", None),
        P(("dp", "sp"), None),
    )
    return jax.shard_map(local, mesh=mesh, in_specs=in_specs, out_specs=out_specs, check_vma=False)
```

```python
import functools
import math

import jax
import jax.numpy as jnp
from jax import lax
from jax.experimental import pallas as pl
from jax.experimental.pallas import tpu as pltpu
from jax.sharding import PartitionSpec as P

HD = 128
NEG = -1e30
BF = jnp.bfloat16
F32 = jnp.float32
NT = (((1,), (1,)), ((), ()))
TN = (((0,), (0,)), ((), ()))
NN = (((1,), (0,)), ((), ()))
MIB = 1024 * 1024
VM = pl.BlockSpec(memory_space=pltpu.VMEM)
SM = pl.BlockSpec(memory_space=pltpu.SMEM)
HB = pl.BlockSpec(memory_space=pltpu.HBM)


def dot(a, b, dims):
    return lax.dot_general(a, b, dims, preferred_element_type=F32)


def ring_order(count):
    return list(range(0, count, 2)) + list(range(1, count, 2))[::-1]


def rows_at(index, size):
    return pl.ds(pl.multiple_of(index * size, size), size)


def grant(mib):
    return pltpu.CompilerParams(vmem_limit_bytes=mib * MIB)


def column_steps(dp, width):
    return max(1, min(4, dp * width // 128 // 2))


def split_kernel(sp, steps, reps, width, base, idx_ref, x_ref, *rest):
    outs, (hold, part, sems) = rest[:sp], rest[sp:]
    block = reps * width
    copies = [
        pltpu.make_async_copy(
            x_ref.at[:, i * sp * block : (i + 1) * sp * block], hold.at[i], sems.at[i]
        )
        for i in range(steps)
    ]
    for copy in copies:
        copy.start()
    for i, copy in enumerate(copies):
        copy.wait()
        for a in range(sp):
            for d in range(reps):
                part[a, :, d * width : (d + 1) * width] = hold[
                    i, :, (d * sp + a) * width : (d * sp + a + 1) * width
                ]
        for r in range(sp):
            outs[r][:, i * block : (i + 1) * block] = part[idx_ref[base + r]]


def split_columns(idx, base, x, sp, dp, width):
    tok = x.shape[0]
    steps = column_steps(dp, width)
    reps = dp // steps
    block = reps * width
    return pl.pallas_call(
        functools.partial(split_kernel, sp, steps, reps, width, base),
        out_shape=[jax.ShapeDtypeStruct((tok, dp * width), BF)] * sp,
        in_specs=[SM, HB],
        out_specs=[VM] * sp,
        scratch_shapes=[
            pltpu.VMEM((steps, tok, sp * block), BF),
            pltpu.VMEM((sp, tok, block), BF),
            pltpu.SemaphoreType.DMA((steps,)),
        ],
        compiler_params=grant(12),
        cost_estimate=pl.CostEstimate(flops=0, bytes_accessed=4 * x.size, transcendentals=0),
        name="split_columns",
    )(idx, pltpu.with_memory_space_constraint(x, pltpu.HBM))


def join_kernel(sp, reps, width, base, idx_ref, *rest):
    ins, out, hold = rest[:sp], rest[sp], rest[sp + 1]
    block = reps * width
    at = pl.ds(pl.multiple_of(pl.program_id(0) * block, block), block)
    for r in range(sp):
        hold[idx_ref[base + r]] = ins[r][:, at]
    for a in range(sp):
        for d in range(reps):
            out[:, (d * sp + a) * width : (d * sp + a + 1) * width] = hold[
                a, :, d * width : (d + 1) * width
            ]


def join_columns(idx, base, pieces, sp, dp, width):
    tok = pieces[0].shape[0]
    steps = column_steps(dp, width)
    reps = dp // steps
    block = reps * width
    return pl.pallas_call(
        functools.partial(join_kernel, sp, reps, width, base),
        out_shape=jax.ShapeDtypeStruct((tok, sp * dp * width), BF),
        grid_spec=pltpu.PrefetchScalarGridSpec(
            num_scalar_prefetch=1,
            grid=(steps,),
            in_specs=[VM] * sp,
            out_specs=pl.BlockSpec((tok, sp * block), lambda d, _: (0, d)),
            scratch_shapes=[pltpu.VMEM((sp, tok, block), BF)],
        ),
        compiler_params=grant(12),
        cost_estimate=pl.CostEstimate(
            flops=0, bytes_accessed=4 * tok * sp * dp * width, transcendentals=0
        ),
        name="join_columns",
    )(idx, *pieces)


def block_kernel(tok, key_ref, doc_ref, out, docs, sems):
    keys = pltpu.make_async_copy(key_ref, out.at[0:tok, :], sems.at[0])
    ids = pltpu.make_async_copy(doc_ref, docs, sems.at[1])
    keys.start()
    ids.start()
    out[tok : tok + 16, :] = jnp.zeros((16, out.shape[1]), BF)
    ids.wait()
    out[tok : tok + 16, 0:tok] = jnp.broadcast_to(docs[...].astype(F32), (16, tok)).astype(BF)
    keys.wait()


def key_block(keys, docs):
    tok, kv = keys.shape
    return pl.pallas_call(
        functools.partial(block_kernel, tok),
        out_shape=jax.ShapeDtypeStruct((tok + 16, kv), BF),
        in_specs=[HB, HB],
        out_specs=VM,
        scratch_shapes=[pltpu.VMEM((1, tok), jnp.int32), pltpu.SemaphoreType.DMA((2,))],
        compiler_params=grant(4),
        cost_estimate=pl.CostEstimate(flops=0, bytes_accessed=4 * keys.size, transcendentals=0),
        name="key_block",
    )(
        pltpu.with_memory_space_constraint(keys, pltpu.HBM),
        pltpu.with_memory_space_constraint(docs, pltpu.HBM),
    )


def fill_keys(sp, tok, win, heads, idx_ref, kd_refs, key_hold, doc_hold, bias):
    first = jnp.maximum(idx_ref[0] + 1 - win, 0)
    head = pl.program_id(0)
    at = pl.ds(pl.multiple_of(head * HD, HD), HD)
    for r in range(sp):
        key_hold[rows_at(idx_ref[r], tok), :] = kd_refs[r][0:tok, at]

    @pl.when(head == 0)
    def _():
        for r in range(sp):
            doc_hold[idx_ref[r]] = kd_refs[r][tok : tok + 16, 0:tok].astype(F32)
        own = jnp.broadcast_to(doc_hold[idx_ref[0]][0:1, :], (tok, tok))
        query_at = idx_ref[0] * tok + lax.broadcasted_iota(jnp.int32, (tok, tok), 1)
        for b in range(win):
            docs = jnp.broadcast_to(doc_hold[first + b][0:1, :], (tok, tok)).T
            key_at = (first + b) * tok + lax.broadcasted_iota(jnp.int32, (tok, tok), 0)
            ok = (key_at <= query_at) & (docs == own)
            block = jnp.where(ok, F32(0.0), F32(NEG))
            for h in range(heads):
                bias[b * tok : (b + 1) * tok, h * tok : (h + 1) * tok] = block

    return first, at


def stack_heads(src, dst, tok, group):
    for h in range(group):
        dst[h * tok : (h + 1) * tok, :] = src[:, h * HD : (h + 1) * HD]


def emit_rel(acc, first, value, sp, tok, win, at, idx_ref, keep, send):
    nx = sp // 2
    acc[...] = jnp.zeros_like(acc)
    acc[pl.ds(pl.multiple_of(first * tok, tok), win * tok), :] = value
    for dx in range(nx):
        keep[dx, :, at] = acc[rows_at(idx_ref[dx], tok), :]
        send[dx, :, at] = acc[rows_at(idx_ref[nx + dx], tok), :]


def probs_kernel(sp, tok, win, group, pair, idx_ref, q_ref, g_ref, *rest):
    kds, (keep, send, lse_ref) = rest[:sp], rest[sp : sp + 3]
    key_hold, doc_hold, bias, q_st, g_st, p_st, acc = rest[sp + 3 :]
    first, cols = fill_keys(sp, tok, win, pair, idx_ref, kds, key_hold, doc_hold, bias)
    factor = F32(HD**-0.5 * math.log2(math.e))
    stack_heads(q_ref, q_st, tok, group)
    stack_heads(g_ref, g_st, tok, group)
    keys = key_hold[pl.ds(pl.multiple_of(first * tok, tok), win * tok), :]
    for h in range(0, group, pair):
        at = slice(h * tok, (h + pair) * tok)
        s = dot(keys, q_st[at, :], NT) * factor + bias[...]
        top = jnp.max(s, axis=0, keepdims=True)
        e = jnp.exp2(s - top)
        total = jnp.sum(e, axis=0, keepdims=True)
        p_st[:, at] = (e * (1.0 / total)).astype(BF)
        lse = top + jnp.log2(total)
        for i in range(pair):
            lse_ref[h + i : h + i + 1, :] = lse[:, i * tok : (i + 1) * tok]
    emit_rel(
        acc, first, dot(p_st[...], g_st[...], NN), sp, tok, win, cols, idx_ref, keep, send
    )


def probs_call(idx, q, g, kds, sp, tok, win, kvh, group):
    nx, seq, pair = sp // 2, sp * tok, 2
    part = jax.ShapeDtypeStruct((nx, tok, kvh * HD), F32)
    wide = pl.BlockSpec((tok, group * HD), lambda c, _: (0, c))
    return pl.pallas_call(
        functools.partial(probs_kernel, sp, tok, win, group, pair),
        out_shape=[part, part, jax.ShapeDtypeStruct((kvh * group, tok), F32)],
        grid_spec=pltpu.PrefetchScalarGridSpec(
            num_scalar_prefetch=1,
            grid=(kvh,),
            in_specs=[wide, wide] + [VM] * sp,
            out_specs=[VM, VM, pl.BlockSpec((group, tok), lambda c, _: (c, 0))],
            scratch_shapes=[
                pltpu.VMEM((seq, HD), BF),
                pltpu.VMEM((sp, 16, tok), F32),
                pltpu.VMEM((win * tok, pair * tok), F32),
                pltpu.VMEM((group * tok, HD), BF),
                pltpu.VMEM((group * tok, HD), BF),
                pltpu.VMEM((win * tok, group * tok), BF),
                pltpu.VMEM((seq, HD), F32),
            ],
        ),
        compiler_params=grant(20),
        cost_estimate=pl.CostEstimate(
            flops=4 * tok * win * tok * kvh * group * HD,
            bytes_accessed=8 * MIB,
            transcendentals=tok * win * tok * kvh * group,
        ),
        name="probs_dv",
    )(idx, q, g, *kds)


def scores_kernel(sp, tok, win, group, pair, idx_ref, q_ref, g_ref, lse_ref, v0_ref, v1_ref, *rest):
    nx = sp // 2
    kds, (dq_ref, keep, send) = rest[:sp], rest[sp : sp + 3]
    key_hold, doc_hold, bias, val_hold, q_st, g_st, ds_st, acc = rest[sp + 3 :]
    first, cols = fill_keys(sp, tok, win, pair, idx_ref, kds, key_hold, doc_hold, bias)
    for dx in range(nx):
        val_hold[rows_at(idx_ref[dx], tok), :] = v0_ref[dx, :, cols]
        val_hold[rows_at(idx_ref[nx + dx], tok), :] = v1_ref[dx, :, cols]
    scale = HD**-0.5
    factor = F32(scale * math.log2(math.e))
    stack_heads(q_ref, q_st, tok, group)
    stack_heads(g_ref, g_st, tok, group)
    window = pl.ds(pl.multiple_of(first * tok, tok), win * tok)
    keys, vals = key_hold[window, :], val_hold[window, :]
    for h in range(0, group, pair):
        at = slice(h * tok, (h + pair) * tok)
        lse = jnp.concatenate([lse_ref[h + i : h + i + 1, :] for i in range(pair)], axis=1)
        shift = lse - F32(math.log2(scale))
        s = dot(keys, q_st[at, :], NT) * factor + bias[...]
        scaled = jnp.exp2(s - shift)
        dp = dot(vals, g_st[at, :], NT)
        delta = jnp.sum(scaled * dp, axis=0, keepdims=True) * F32(1.0 / scale)
        ds_st[:, at] = (scaled * (dp - delta)).astype(BF)
    dq = dot(ds_st[...], keys, TN)
    for h in range(group):
        dq_ref[:, h * HD : (h + 1) * HD] = dq[h * tok : (h + 1) * tok, :].astype(BF)
    emit_rel(
        acc, first, dot(ds_st[...], q_st[...], NN), sp, tok, win, cols, idx_ref, keep, send
    )


def scores_call(idx, q, g, lse, v0, v1, kds, sp, tok, win, kvh, group):
    nx, seq, pair = sp // 2, sp * tok, 2
    part = jax.ShapeDtypeStruct((nx, tok, kvh * HD), F32)
    wide = pl.BlockSpec((tok, group * HD), lambda c, _: (0, c))
    return pl.pallas_call(
        functools.partial(scores_kernel, sp, tok, win, group, pair),
        out_shape=[jax.ShapeDtypeStruct(q.shape, BF), part, part],
        grid_spec=pltpu.PrefetchScalarGridSpec(
            num_scalar_prefetch=1,
            grid=(kvh,),
            in_specs=[wide, wide, pl.BlockSpec((group, tok), lambda c, _: (c, 0)), VM, VM]
            + [VM] * sp,
            out_specs=[wide, VM, VM],
            scratch_shapes=[
                pltpu.VMEM((seq, HD), BF),
                pltpu.VMEM((sp, 16, tok), F32),
                pltpu.VMEM((win * tok, pair * tok), F32),
                pltpu.VMEM((seq, HD), BF),
                pltpu.VMEM((group * tok, HD), BF),
                pltpu.VMEM((group * tok, HD), BF),
                pltpu.VMEM((win * tok, group * tok), BF),
                pltpu.VMEM((seq, HD), F32),
            ],
        ),
        compiler_params=grant(24),
        cost_estimate=pl.CostEstimate(
            flops=8 * tok * win * tok * kvh * group * HD,
            bytes_accessed=10 * MIB,
            transcendentals=tok * win * tok * kvh * group,
        ),
        name="scores_dq_dk",
    )(idx, q, g, lse, v0, v1, *kds)


def values_kernel(sp, dp, tok, width, base, idx_ref, *rest):
    nx = sp // 2
    xs, ws = rest[:sp], rest[sp : sp + dp]
    keep, send, x_hold, w_hold = rest[sp + dp :]
    for i in range(dp):
        w_hold[rows_at(idx_ref[base + i], width), :] = ws[i][...]
    for r in range(sp):
        x_hold[r * tok : (r + 1) * tok, :] = xs[r][...]
    out = dot(x_hold[...], w_hold[...], NN)
    for dx in range(nx):
        keep[dx] = out[dx * tok : (dx + 1) * tok]
        send[dx] = out[(nx + dx) * tok : (nx + dx + 1) * tok]


def values_call(idx, base, xs, ws, sp, dp, tok, width):
    nx, kv = sp // 2, ws[0].shape[1]
    cols = dp * width
    part = jax.ShapeDtypeStruct((nx, tok, kv), F32)
    return pl.pallas_call(
        functools.partial(values_kernel, sp, dp, tok, width, base),
        out_shape=[part, part],
        in_specs=[SM] + [VM] * (sp + dp),
        out_specs=[VM] * 2,
        scratch_shapes=[pltpu.VMEM((sp * tok, cols), BF), pltpu.VMEM((cols, kv), BF)],
        compiler_params=grant(16),
        cost_estimate=pl.CostEstimate(
            flops=2 * sp * tok * cols * kv, bytes_accessed=8 * MIB, transcendentals=0
        ),
        name="values_part",
    )(idx, *xs, *ws)


def wgrad_kernel(sp, nz, ny, tok, width, base, idx_ref, *rest):
    nx = sp // 2
    xs, (g0, g1) = rest[:sp], rest[sp : sp + 2]
    outs = rest[sp + 2 : sp + 2 + 2 * nz]
    x_hold, g_hold, total = rest[sp + 2 + 2 * nz :]
    for dx in range(nx):
        for core, src in ((0, g0), (1, g1)):
            r = core * nx + dx
            x_hold[r * tok : (r + 1) * tok, :] = xs[r][...]
            g_hold[r * tok : (r + 1) * tok, :] = src[dx]
    cols = x_hold.shape[1]
    step = min(cols, 512)
    for at in range(0, cols, step):
        total[at : at + step, :] = dot(x_hold[:, at : at + step], g_hold[...], TN)
    for k in range(nz):
        outs[k][...] = total[rows_at(idx_ref[base + k * ny], width), :].astype(BF)
        for j in range(1, ny):
            outs[nz + k][j - 1] = total[rows_at(idx_ref[base + k * ny + j], width), :]


def wgrad_call(idx, base, xs, g0, g1, sp, nz, ny, tok, width):
    kv = g0.shape[2]
    cols = nz * ny * width
    return pl.pallas_call(
        functools.partial(wgrad_kernel, sp, nz, ny, tok, width, base),
        out_shape=[jax.ShapeDtypeStruct((width, kv), BF)] * nz
        + [jax.ShapeDtypeStruct((ny - 1, width, kv), F32)] * nz,
        in_specs=[SM] + [VM] * (sp + 2),
        out_specs=[VM] * (2 * nz),
        scratch_shapes=[
            pltpu.VMEM((sp * tok, cols), BF),
            pltpu.VMEM((sp * tok, kv), BF),
            pltpu.VMEM((cols, kv), F32),
        ],
        compiler_params=grant(20),
        cost_estimate=pl.CostEstimate(
            flops=2 * sp * tok * cols * kv, bytes_accessed=7 * MIB, transcendentals=0
        ),
        name="weight_grad_part",
    )(idx, *xs, g0, g1)


def igrad_kernel(sp, dp, tok, width, base, idx_ref, g0, g1, *rest):
    nx = sp // 2
    ws, outs = rest[:dp], rest[dp : dp + sp]
    g_hold, w_hold = rest[dp + sp :]
    for i in range(dp):
        w_hold[rows_at(idx_ref[base + i], width), :] = ws[i][...]
    for dx in range(nx):
        g_hold[dx * tok : (dx + 1) * tok, :] = g0[dx]
        g_hold[(nx + dx) * tok : (nx + dx + 1) * tok, :] = g1[dx]
    cols = w_hold.shape[0]
    step = min(cols, 512)
    for at in range(0, cols, step):
        out = dot(g_hold[...], w_hold[at : at + step, :], NT)
        for r in range(sp):
            outs[r][:, at : at + step] = out[r * tok : (r + 1) * tok].astype(BF)


def igrad_call(idx, base, g0, g1, ws, sp, dp, tok, width):
    kv = g0.shape[2]
    cols = dp * width
    return pl.pallas_call(
        functools.partial(igrad_kernel, sp, dp, tok, width, base),
        out_shape=[jax.ShapeDtypeStruct((tok, cols), BF)] * sp,
        in_specs=[SM] + [VM] * (2 + dp),
        out_specs=[VM] * sp,
        scratch_shapes=[pltpu.VMEM((sp * tok, kv), BF), pltpu.VMEM((cols, kv), BF)],
        compiler_params=grant(16),
        cost_estimate=pl.CostEstimate(
            flops=2 * sp * tok * cols * kv, bytes_accessed=5 * MIB, transcendentals=0
        ),
        name="input_grad_part",
    )(idx, g0, g1, *ws)


def after(value, *others):
    return lax.optimization_barrier((value, *others))[0]


def local(layer_input, value_weight, query_states, key_states, out_grad, doc_ids):
    sp, dp = lax.axis_size("sp"), lax.axis_size("dp")
    nx = sp // 2
    ny = max(1, min(nx, dp))
    nz = dp // ny
    tok = layer_input.shape[1]
    width = value_weight.shape[0]
    kvh = key_states.shape[2] // HD
    group = query_states.shape[2] // HD // kvh
    win = min(sp, sp // 2 + 1)

    def sp_perm(dx, dc):
        return [(i, ((i // 2 + dx) % nx) * 2 + (i % 2 ^ dc)) for i in range(sp)]

    def send_sp(v, dx, dc):
        return lax.ppermute(v, "sp", sp_perm(dx % nx, dc))

    z_ring, y_ring = ring_order(nz), ring_order(ny)

    def pred(ring, at, k):
        return ring[(ring.index(at) - k) % len(ring)]

    z_next = [
        (z_ring[p] * ny + y, z_ring[(p + 1) % nz] * ny + y) for p in range(nz) for y in range(ny)
    ]
    z_back = [(j, i) for i, j in z_next]
    ahead = nz // 2
    behind = nz - 1 - ahead
    y_next = [
        (z * ny + y_ring[p], z * ny + y_ring[(p + 1) % ny]) for p in range(ny) for z in range(nz)
    ]

    def send_z(v, forward=True):
        return lax.ppermute(v, "dp", z_next if forward else z_back)

    def send_y(v):
        return lax.ppermute(v, "dp", y_next)

    from_z = [0, *range(1, ahead + 1), *(-k for k in range(1, behind + 1))]
    to_z = sorted(from_z, key=lambda k: (-abs(k), -k))

    table = []
    for d in range(dp):
        z, y = d // ny, d % ny
        for s in range(sp):
            x, core = s // 2, s % 2
            row = [((x - dx) % nx) * 2 + (core ^ dc) for dc in range(2) for dx in range(nx)]
            row += [((x + dx) % nx) * 2 + (core ^ dc) for dc in range(2) for dx in range(nx)]
            row += [
                pred(z_ring, z, k) * ny + pred(y_ring, y, j) for k in from_z for j in range(ny)
            ]
            row += [
                pred(z_ring, z, -k) * ny + pred(y_ring, y, j)
                for k in to_z
                for j in range(1, ny + 1)
            ]
            table.append(row)
    at_fwd, at_gather, at_scatter = sp, 2 * sp, 2 * sp + dp
    flat = lax.axis_index("dp") * sp + lax.axis_index("sp")
    idx = lax.dynamic_index_in_dim(jnp.asarray(table, jnp.int32), flat, 0, keepdims=False)

    q, g = query_states[0], out_grad[0]

    kd = key_block(key_states[0], doc_ids)
    near = [kd] + [send_sp(kd, dx, 0) for dx in range(1, nx)]
    kds = near + [send_sp(v, 0, 1) for v in near]

    z_rows = [value_weight]
    for _ in range(1, ahead + 1):
        z_rows.append(send_z(z_rows[-1]))
    for k in range(1, behind + 1):
        z_rows.append(send_z(z_rows[-1] if k > 1 else value_weight, False))
    rows = []
    for v in z_rows:
        for j in range(ny):
            rows.append(v)
            if j + 1 < ny:
                v = send_y(v)

    pieces = split_columns(idx, at_fwd, layer_input[0], sp, dp, width)
    ready = [pieces[0]] + [after(v, near[-1]) for v in pieces[1:]]

    dv_keep, dv_send, lse = probs_call(idx, q, g, kds, sp, tok, win, kvh, group)

    def reduce_core(keep, send):
        return keep + send_sp(send, 0, 1)

    def reduce_all(keep, send):
        here = reduce_core(keep, send)
        small = here.astype(BF)
        total, got = here, small
        for k in range(1, nx):
            got = send_sp(small, k, 0)
            total = total + jnp.roll(got, k, axis=0).astype(F32)
        mine = total.astype(BF)
        return mine, send_sp(mine, 0, 1), got

    vg0, vg1, _ = reduce_all(dv_keep, dv_send)

    xs = [pieces[0]]
    for r in range(1, sp):
        dx, dc = r % nx, r // nx
        xs.append(send_sp(ready[r], dx, dc))

    parts = igrad_call(idx, at_gather, vg0, vg1, rows, sp, dp, tok, width)

    blocks = wgrad_call(idx, at_scatter, xs, vg0, vg1, sp, nz, ny, tok, width)
    lines = {}
    for i, k in enumerate(to_z):
        line = blocks[i]
        for j in range(1, ny):
            line = send_y(line.astype(BF)).astype(F32) + blocks[nz + i][j - 1]
        lines[k] = line.astype(F32)
    weight_grad = lines[0]
    for count, sign in ((ahead, 1), (behind, -1)):
        run = None
        for k in range(count, 0, -1):
            run = lines[sign * k] if run is None else run + lines[sign * k]
            run = send_z(run.astype(BF), sign > 0).astype(F32)
        if run is not None:
            weight_grad = weight_grad + run

    v_keep, v_send = values_call(idx, at_gather, xs, rows, sp, dp, tok, width)
    v0, v1, v_got = reduce_all(v_keep, v_send)
    dq, dk_keep, dk_send = scores_call(idx, q, g, lse, v0, v1, kds, sp, tok, win, kvh, group)
    dk = reduce_core(dk_keep, dk_send)
    key_sum = dk[0]
    for k in range(1, nx):
        key_sum = key_sum + send_sp(dk[-k % nx].astype(BF), k, 0).astype(F32)
    key_grad = key_sum.astype(BF)

    back = [parts[0]]
    for r in range(1, sp):
        dx, dc = r % nx, r // nx
        if dx and dc:
            back.append(send_sp(after(parts[r], v_got), -dx, dc))
        else:
            back.append(send_sp(parts[r], -dx, dc))
    input_grad = join_columns(idx, at_fwd, back, sp, dp, width)

    return (dq[None], key_grad[None], input_grad[None], weight_grad)


def solution(mesh):
    in_specs = (
        P("dp", "sp", None),
        P(("dp", "sp"), None),
        P("dp", "sp", None),
        P("dp", "sp", None),
        P("dp", "sp", None),
        P("dp", "sp"),
    )
    out_specs = (
        P("dp", "sp", None),
        P("dp", "sp", None),
        P("dp", "sp", None),
        P(("dp", "sp"), None),
    )
    return jax.shard_map(local, mesh=mesh, in_specs=in_specs, out_specs=out_specs, check_vma=False)
```

```python
import functools
import math

import jax
import jax.numpy as jnp
from jax import lax
from jax.experimental import pallas as pl
from jax.experimental.pallas import tpu as pltpu
from jax.sharding import PartitionSpec as P

HD = 128
NEG = -1e30
BF = jnp.bfloat16
F32 = jnp.float32
NT = (((1,), (1,)), ((), ()))
TN = (((0,), (0,)), ((), ()))
NN = (((1,), (0,)), ((), ()))
MIB = 1024 * 1024
VM = pl.BlockSpec(memory_space=pltpu.VMEM)
SM = pl.BlockSpec(memory_space=pltpu.SMEM)
HB = pl.BlockSpec(memory_space=pltpu.HBM)


def dot(a, b, dims):
    return lax.dot_general(a, b, dims, preferred_element_type=F32)


def ring_order(count):
    return list(range(0, count, 2)) + list(range(1, count, 2))[::-1]


def rows_at(index, size):
    return pl.ds(pl.multiple_of(index * size, size), size)


def grant(mib):
    return pltpu.CompilerParams(vmem_limit_bytes=mib * MIB)


def column_steps(dp, width):
    return max(1, min(4, dp * width // 128 // 2))


def split_kernel(sp, steps, reps, width, base, idx_ref, x_ref, *rest):
    outs, (hold, part, sems) = rest[:sp], rest[sp:]
    block = reps * width
    copies = [
        pltpu.make_async_copy(
            x_ref.at[:, i * sp * block : (i + 1) * sp * block], hold.at[i], sems.at[i]
        )
        for i in range(steps)
    ]
    for copy in copies:
        copy.start()
    for i, copy in enumerate(copies):
        copy.wait()
        for a in range(sp):
            for d in range(reps):
                part[a, :, d * width : (d + 1) * width] = hold[
                    i, :, (d * sp + a) * width : (d * sp + a + 1) * width
                ]
        for r in range(sp):
            outs[r][:, i * block : (i + 1) * block] = part[idx_ref[base + r]]


def split_columns(idx, base, x, sp, dp, width):
    tok = x.shape[0]
    steps = column_steps(dp, width)
    reps = dp // steps
    block = reps * width
    return pl.pallas_call(
        functools.partial(split_kernel, sp, steps, reps, width, base),
        out_shape=[jax.ShapeDtypeStruct((tok, dp * width), BF)] * sp,
        in_specs=[SM, HB],
        out_specs=[VM] * sp,
        scratch_shapes=[
            pltpu.VMEM((steps, tok, sp * block), BF),
            pltpu.VMEM((sp, tok, block), BF),
            pltpu.SemaphoreType.DMA((steps,)),
        ],
        compiler_params=grant(12),
        cost_estimate=pl.CostEstimate(flops=0, bytes_accessed=4 * x.size, transcendentals=0),
        name="split_columns",
    )(idx, pltpu.with_memory_space_constraint(x, pltpu.HBM))


def join_kernel(sp, reps, width, base, idx_ref, *rest):
    ins, out, hold = rest[:sp], rest[sp], rest[sp + 1]
    block = reps * width
    at = pl.ds(pl.multiple_of(pl.program_id(0) * block, block), block)
    for r in range(sp):
        hold[idx_ref[base + r]] = ins[r][:, at]
    for a in range(sp):
        for d in range(reps):
            out[:, (d * sp + a) * width : (d * sp + a + 1) * width] = hold[
                a, :, d * width : (d + 1) * width
            ]


def join_columns(idx, base, pieces, sp, dp, width):
    tok = pieces[0].shape[0]
    steps = column_steps(dp, width)
    reps = dp // steps
    block = reps * width
    return pl.pallas_call(
        functools.partial(join_kernel, sp, reps, width, base),
        out_shape=jax.ShapeDtypeStruct((tok, sp * dp * width), BF),
        grid_spec=pltpu.PrefetchScalarGridSpec(
            num_scalar_prefetch=1,
            grid=(steps,),
            in_specs=[VM] * sp,
            out_specs=pl.BlockSpec((tok, sp * block), lambda d, _: (0, d)),
            scratch_shapes=[pltpu.VMEM((sp, tok, block), BF)],
        ),
        compiler_params=grant(12),
        cost_estimate=pl.CostEstimate(
            flops=0, bytes_accessed=4 * tok * sp * dp * width, transcendentals=0
        ),
        name="join_columns",
    )(idx, *pieces)


def block_kernel(tok, key_ref, doc_ref, out, docs, sems):
    keys = pltpu.make_async_copy(key_ref, out.at[0:tok, :], sems.at[0])
    ids = pltpu.make_async_copy(doc_ref, docs, sems.at[1])
    keys.start()
    ids.start()
    out[tok : tok + 16, :] = jnp.zeros((16, out.shape[1]), BF)
    ids.wait()
    out[tok : tok + 16, 0:tok] = jnp.broadcast_to(docs[...].astype(F32), (16, tok)).astype(BF)
    keys.wait()


def key_block(keys, docs):
    tok, kv = keys.shape
    return pl.pallas_call(
        functools.partial(block_kernel, tok),
        out_shape=jax.ShapeDtypeStruct((tok + 16, kv), BF),
        in_specs=[HB, HB],
        out_specs=VM,
        scratch_shapes=[pltpu.VMEM((1, tok), jnp.int32), pltpu.SemaphoreType.DMA((2,))],
        compiler_params=grant(4),
        cost_estimate=pl.CostEstimate(flops=0, bytes_accessed=4 * keys.size, transcendentals=0),
        name="key_block",
    )(
        pltpu.with_memory_space_constraint(keys, pltpu.HBM),
        pltpu.with_memory_space_constraint(docs, pltpu.HBM),
    )


def fill_keys(sp, tok, win, heads, idx_ref, kd_refs, key_hold, doc_hold, bias):
    first = jnp.maximum(idx_ref[0] + 1 - win, 0)
    head = pl.program_id(0)
    at = pl.ds(pl.multiple_of(head * HD, HD), HD)
    for r in range(sp):
        key_hold[rows_at(idx_ref[r], tok), :] = kd_refs[r][0:tok, at]
    if bias is None:
        return first, at

    @pl.when(head == 0)
    def _():
        for r in range(sp):
            doc_hold[idx_ref[r]] = kd_refs[r][tok : tok + 16, 0:tok].astype(F32)
        own = jnp.broadcast_to(doc_hold[idx_ref[0]][0:1, :], (tok, tok))
        query_at = idx_ref[0] * tok + lax.broadcasted_iota(jnp.int32, (tok, tok), 1)
        for b in range(win):
            docs = jnp.broadcast_to(doc_hold[first + b][0:1, :], (tok, tok)).T
            key_at = (first + b) * tok + lax.broadcasted_iota(jnp.int32, (tok, tok), 0)
            ok = (key_at <= query_at) & (docs == own)
            block = jnp.where(ok, F32(0.0), F32(NEG))
            for h in range(heads):
                bias[b * tok : (b + 1) * tok, h * tok : (h + 1) * tok] = block

    return first, at


def stack_heads(src, dst, tok, group):
    for h in range(group):
        dst[h * tok : (h + 1) * tok, :] = src[:, h * HD : (h + 1) * HD]


def emit_rel(acc, first, value, sp, tok, win, at, idx_ref, keep, send):
    nx = sp // 2
    acc[...] = jnp.zeros_like(acc)
    acc[pl.ds(pl.multiple_of(first * tok, tok), win * tok), :] = value
    for dx in range(nx):
        keep[dx, :, at] = acc[rows_at(idx_ref[dx], tok), :]
        send[dx, :, at] = acc[rows_at(idx_ref[nx + dx], tok), :]


def probs_kernel(sp, tok, win, group, pair, idx_ref, q_ref, g_ref, *rest):
    kds, (keep, send, p_ref) = rest[:sp], rest[sp : sp + 3]
    key_hold, doc_hold, bias, q_st, g_st, acc = rest[sp + 3 :]
    p_st = p_ref.at[pl.program_id(0)]
    first, cols = fill_keys(sp, tok, win, pair, idx_ref, kds, key_hold, doc_hold, bias)
    factor = F32(HD**-0.5 * math.log2(math.e))
    stack_heads(q_ref, q_st, tok, group)
    stack_heads(g_ref, g_st, tok, group)
    keys = key_hold[pl.ds(pl.multiple_of(first * tok, tok), win * tok), :]
    for h in range(0, group, pair):
        at = slice(h * tok, (h + pair) * tok)
        s = dot(keys, q_st[at, :], NT) * factor + bias[...]
        top = jnp.max(s, axis=0, keepdims=True)
        e = jnp.exp2(s - top)
        total = jnp.sum(e, axis=0, keepdims=True)
        p_st[:, at] = (e * (1.0 / total)).astype(BF)
    emit_rel(
        acc, first, dot(p_st[...], g_st[...], NN), sp, tok, win, cols, idx_ref, keep, send
    )


def probs_call(idx, q, g, kds, sp, tok, win, kvh, group):
    nx, seq, pair = sp // 2, sp * tok, 2
    part = jax.ShapeDtypeStruct((nx, tok, kvh * HD), F32)
    wide = pl.BlockSpec((tok, group * HD), lambda c, _: (0, c))
    return pl.pallas_call(
        functools.partial(probs_kernel, sp, tok, win, group, pair),
        out_shape=[part, part, jax.ShapeDtypeStruct((kvh, win * tok, group * tok), BF)],
        grid_spec=pltpu.PrefetchScalarGridSpec(
            num_scalar_prefetch=1,
            grid=(kvh,),
            in_specs=[wide, wide] + [VM] * sp,
            out_specs=[VM, VM, VM],
            scratch_shapes=[
                pltpu.VMEM((seq, HD), BF),
                pltpu.VMEM((sp, 16, tok), F32),
                pltpu.VMEM((win * tok, pair * tok), F32),
                pltpu.VMEM((group * tok, HD), BF),
                pltpu.VMEM((group * tok, HD), BF),
                pltpu.VMEM((seq, HD), F32),
            ],
        ),
        compiler_params=grant(20),
        cost_estimate=pl.CostEstimate(
            flops=4 * tok * win * tok * kvh * group * HD,
            bytes_accessed=8 * MIB,
            transcendentals=tok * win * tok * kvh * group,
        ),
        name="probs_dv",
    )(idx, q, g, *kds)


def scores_kernel(sp, tok, win, group, pair, idx_ref, q_ref, g_ref, p_ref, v0_ref, v1_ref, *rest):
    nx = sp // 2
    kds, (dq_ref, keep, send) = rest[:sp], rest[sp : sp + 3]
    key_hold, val_hold, q_st, g_st, ds_st, acc = rest[sp + 3 :]
    first, cols = fill_keys(sp, tok, win, pair, idx_ref, kds, key_hold, None, None)
    for dx in range(nx):
        val_hold[rows_at(idx_ref[dx], tok), :] = v0_ref[dx, :, cols]
        val_hold[rows_at(idx_ref[nx + dx], tok), :] = v1_ref[dx, :, cols]
    scale = F32(HD**-0.5)
    stack_heads(q_ref, q_st, tok, group)
    stack_heads(g_ref, g_st, tok, group)
    window = pl.ds(pl.multiple_of(first * tok, tok), win * tok)
    keys, vals = key_hold[window, :], val_hold[window, :]
    p_st = p_ref.at[pl.program_id(0)]
    for h in range(0, group, pair):
        at = slice(h * tok, (h + pair) * tok)
        dp = dot(vals, g_st[at, :], NT)
        probs = p_st[:, at].astype(F32)
        delta = jnp.sum(probs * dp, axis=0, keepdims=True)
        ds_st[:, at] = (probs * (dp - delta)).astype(BF)
    dq = dot(ds_st[...], keys, TN) * scale
    for h in range(group):
        dq_ref[:, h * HD : (h + 1) * HD] = dq[h * tok : (h + 1) * tok, :].astype(BF)
    dk = dot(ds_st[...], q_st[...], NN) * scale
    emit_rel(acc, first, dk, sp, tok, win, cols, idx_ref, keep, send)


def scores_call(idx, q, g, p, v0, v1, kds, sp, tok, win, kvh, group):
    nx, seq, pair = sp // 2, sp * tok, 2
    part = jax.ShapeDtypeStruct((nx, tok, kvh * HD), F32)
    wide = pl.BlockSpec((tok, group * HD), lambda c, _: (0, c))
    return pl.pallas_call(
        functools.partial(scores_kernel, sp, tok, win, group, pair),
        out_shape=[jax.ShapeDtypeStruct(q.shape, BF), part, part],
        grid_spec=pltpu.PrefetchScalarGridSpec(
            num_scalar_prefetch=1,
            grid=(kvh,),
            in_specs=[wide, wide] + [VM] * (3 + sp),
            out_specs=[wide, VM, VM],
            scratch_shapes=[
                pltpu.VMEM((seq, HD), BF),
                pltpu.VMEM((seq, HD), BF),
                pltpu.VMEM((group * tok, HD), BF),
                pltpu.VMEM((group * tok, HD), BF),
                pltpu.VMEM((win * tok, group * tok), BF),
                pltpu.VMEM((seq, HD), F32),
            ],
        ),
        compiler_params=grant(24),
        cost_estimate=pl.CostEstimate(
            flops=6 * tok * win * tok * kvh * group * HD,
            bytes_accessed=10 * MIB,
            transcendentals=0,
        ),
        name="scores_dq_dk",
    )(idx, q, g, p, v0, v1, *kds)


def values_kernel(sp, dp, tok, width, base, idx_ref, *rest):
    nx = sp // 2
    xs, ws = rest[:sp], rest[sp : sp + dp]
    keep, send, x_hold, w_hold = rest[sp + dp :]
    for i in range(dp):
        w_hold[rows_at(idx_ref[base + i], width), :] = ws[i][...]
    for r in range(sp):
        x_hold[r * tok : (r + 1) * tok, :] = xs[r][...]
    out = dot(x_hold[...], w_hold[...], NN)
    for dx in range(nx):
        keep[dx] = out[dx * tok : (dx + 1) * tok]
        send[dx] = out[(nx + dx) * tok : (nx + dx + 1) * tok]


def values_call(idx, base, xs, ws, sp, dp, tok, width):
    nx, kv = sp // 2, ws[0].shape[1]
    cols = dp * width
    part = jax.ShapeDtypeStruct((nx, tok, kv), F32)
    return pl.pallas_call(
        functools.partial(values_kernel, sp, dp, tok, width, base),
        out_shape=[part, part],
        in_specs=[SM] + [VM] * (sp + dp),
        out_specs=[VM] * 2,
        scratch_shapes=[pltpu.VMEM((sp * tok, cols), BF), pltpu.VMEM((cols, kv), BF)],
        compiler_params=grant(16),
        cost_estimate=pl.CostEstimate(
            flops=2 * sp * tok * cols * kv, bytes_accessed=8 * MIB, transcendentals=0
        ),
        name="values_part",
    )(idx, *xs, *ws)


def wgrad_kernel(sp, nz, ny, tok, width, base, idx_ref, *rest):
    nx = sp // 2
    xs, (g0, g1) = rest[:sp], rest[sp : sp + 2]
    outs = rest[sp + 2 : sp + 2 + 2 * nz]
    x_hold, g_hold, total = rest[sp + 2 + 2 * nz :]
    for dx in range(nx):
        for core, src in ((0, g0), (1, g1)):
            r = core * nx + dx
            x_hold[r * tok : (r + 1) * tok, :] = xs[r][...]
            g_hold[r * tok : (r + 1) * tok, :] = src[dx]
    cols = x_hold.shape[1]
    step = min(cols, 512)
    for at in range(0, cols, step):
        total[at : at + step, :] = dot(x_hold[:, at : at + step], g_hold[...], TN)
    for k in range(nz):
        outs[k][...] = total[rows_at(idx_ref[base + k * ny], width), :].astype(BF)
        for j in range(1, ny):
            outs[nz + k][j - 1] = total[rows_at(idx_ref[base + k * ny + j], width), :]


def wgrad_call(idx, base, xs, g0, g1, sp, nz, ny, tok, width):
    kv = g0.shape[2]
    cols = nz * ny * width
    return pl.pallas_call(
        functools.partial(wgrad_kernel, sp, nz, ny, tok, width, base),
        out_shape=[jax.ShapeDtypeStruct((width, kv), BF)] * nz
        + [jax.ShapeDtypeStruct((ny - 1, width, kv), F32)] * nz,
        in_specs=[SM] + [VM] * (sp + 2),
        out_specs=[VM] * (2 * nz),
        scratch_shapes=[
            pltpu.VMEM((sp * tok, cols), BF),
            pltpu.VMEM((sp * tok, kv), BF),
            pltpu.VMEM((cols, kv), F32),
        ],
        compiler_params=grant(20),
        cost_estimate=pl.CostEstimate(
            flops=2 * sp * tok * cols * kv, bytes_accessed=7 * MIB, transcendentals=0
        ),
        name="weight_grad_part",
    )(idx, *xs, g0, g1)


def igrad_kernel(sp, dp, tok, width, base, idx_ref, g0, g1, *rest):
    nx = sp // 2
    ws, outs = rest[:dp], rest[dp : dp + sp]
    g_hold, w_hold = rest[dp + sp :]
    for i in range(dp):
        w_hold[rows_at(idx_ref[base + i], width), :] = ws[i][...]
    for dx in range(nx):
        g_hold[dx * tok : (dx + 1) * tok, :] = g0[dx]
        g_hold[(nx + dx) * tok : (nx + dx + 1) * tok, :] = g1[dx]
    cols = w_hold.shape[0]
    step = min(cols, 512)
    for at in range(0, cols, step):
        out = dot(g_hold[...], w_hold[at : at + step, :], NT)
        for r in range(sp):
            outs[r][:, at : at + step] = out[r * tok : (r + 1) * tok].astype(BF)


def igrad_call(idx, base, g0, g1, ws, sp, dp, tok, width):
    kv = g0.shape[2]
    cols = dp * width
    return pl.pallas_call(
        functools.partial(igrad_kernel, sp, dp, tok, width, base),
        out_shape=[jax.ShapeDtypeStruct((tok, cols), BF)] * sp,
        in_specs=[SM] + [VM] * (2 + dp),
        out_specs=[VM] * sp,
        scratch_shapes=[pltpu.VMEM((sp * tok, kv), BF), pltpu.VMEM((cols, kv), BF)],
        compiler_params=grant(16),
        cost_estimate=pl.CostEstimate(
            flops=2 * sp * tok * cols * kv, bytes_accessed=5 * MIB, transcendentals=0
        ),
        name="input_grad_part",
    )(idx, g0, g1, *ws)


def after(value, *others):
    return lax.optimization_barrier((value, *others))[0]


def local(layer_input, value_weight, query_states, key_states, out_grad, doc_ids):
    sp, dp = lax.axis_size("sp"), lax.axis_size("dp")
    nx = sp // 2
    ny = max(1, min(nx, dp))
    nz = dp // ny
    tok = layer_input.shape[1]
    width = value_weight.shape[0]
    kvh = key_states.shape[2] // HD
    group = query_states.shape[2] // HD // kvh
    win = min(sp, sp // 2 + 1)

    def sp_perm(dx, dc):
        return [(i, ((i // 2 + dx) % nx) * 2 + (i % 2 ^ dc)) for i in range(sp)]

    def send_sp(v, dx, dc):
        return lax.ppermute(v, "sp", sp_perm(dx % nx, dc))

    z_ring, y_ring = ring_order(nz), ring_order(ny)

    def pred(ring, at, k):
        return ring[(ring.index(at) - k) % len(ring)]

    z_next = [
        (z_ring[p] * ny + y, z_ring[(p + 1) % nz] * ny + y) for p in range(nz) for y in range(ny)
    ]
    z_back = [(j, i) for i, j in z_next]
    ahead = nz // 2
    behind = nz - 1 - ahead
    y_next = [
        (z * ny + y_ring[p], z * ny + y_ring[(p + 1) % ny]) for p in range(ny) for z in range(nz)
    ]

    def send_z(v, forward=True):
        return lax.ppermute(v, "dp", z_next if forward else z_back)

    def send_y(v):
        return lax.ppermute(v, "dp", y_next)

    from_z = [0, *range(1, ahead + 1), *(-k for k in range(1, behind + 1))]
    to_z = sorted(from_z, key=lambda k: (-abs(k), -k))

    table = []
    for d in range(dp):
        z, y = d // ny, d % ny
        for s in range(sp):
            x, core = s // 2, s % 2
            row = [((x - dx) % nx) * 2 + (core ^ dc) for dc in range(2) for dx in range(nx)]
            row += [((x + dx) % nx) * 2 + (core ^ dc) for dc in range(2) for dx in range(nx)]
            row += [
                pred(z_ring, z, k) * ny + pred(y_ring, y, j) for k in from_z for j in range(ny)
            ]
            row += [
                pred(z_ring, z, -k) * ny + pred(y_ring, y, j)
                for k in to_z
                for j in range(1, ny + 1)
            ]
            table.append(row)
    at_fwd, at_gather, at_scatter = sp, 2 * sp, 2 * sp + dp
    flat = lax.axis_index("dp") * sp + lax.axis_index("sp")
    idx = lax.dynamic_index_in_dim(jnp.asarray(table, jnp.int32), flat, 0, keepdims=False)

    q, g = query_states[0], out_grad[0]

    kd = key_block(key_states[0], doc_ids)
    near = [kd] + [send_sp(kd, dx, 0) for dx in range(1, nx)]
    kds = near + [send_sp(v, 0, 1) for v in near]

    z_rows = [value_weight]
    for _ in range(1, ahead + 1):
        z_rows.append(send_z(z_rows[-1]))
    for k in range(1, behind + 1):
        z_rows.append(send_z(z_rows[-1] if k > 1 else value_weight, False))
    rows = []
    for v in z_rows:
        for j in range(ny):
            rows.append(v)
            if j + 1 < ny:
                v = send_y(v)

    pieces = split_columns(idx, at_fwd, layer_input[0], sp, dp, width)
    ready = [pieces[0]] + [after(v, near[-1]) for v in pieces[1:]]

    dv_keep, dv_send, probs = probs_call(idx, q, g, kds, sp, tok, win, kvh, group)

    def reduce_core(keep, send):
        return keep + send_sp(send, 0, 1)

    def reduce_all(keep, send):
        here = reduce_core(keep, send)
        small = here.astype(BF)
        total, got = here, small
        for k in range(1, nx):
            got = send_sp(small, k, 0)
            total = total + jnp.roll(got, k, axis=0).astype(F32)
        mine = total.astype(BF)
        return mine, send_sp(mine, 0, 1), got

    vg0, vg1, vg_got = reduce_all(dv_keep, dv_send)

    xs = [pieces[0]]
    for r in range(1, sp):
        dx, dc = r % nx, r // nx
        if dx and dc:
            xs.append(send_sp(after(ready[r], vg_got), dx, dc))
        else:
            xs.append(send_sp(ready[r], dx, dc))

    parts = igrad_call(idx, at_gather, vg0, vg1, rows, sp, dp, tok, width)

    blocks = wgrad_call(idx, at_scatter, xs, vg0, vg1, sp, nz, ny, tok, width)
    lines = {}
    for i, k in enumerate(to_z):
        line = blocks[i]
        for j in range(1, ny):
            line = send_y(line.astype(BF)).astype(F32) + blocks[nz + i][j - 1]
        lines[k] = line.astype(F32)
    weight_grad = lines[0]
    for count, sign in ((ahead, 1), (behind, -1)):
        run = None
        for k in range(count, 0, -1):
            run = lines[sign * k] if run is None else run + lines[sign * k]
            run = send_z(run.astype(BF), sign > 0).astype(F32)
        if run is not None:
            weight_grad = weight_grad + run

    v_keep, v_send = values_call(idx, at_gather, xs, rows, sp, dp, tok, width)
    v0, v1, v_got = reduce_all(v_keep, v_send)
    dq, dk_keep, dk_send = scores_call(idx, q, g, probs, v0, v1, kds, sp, tok, win, kvh, group)
    dk = reduce_core(dk_keep, dk_send)
    key_sum = dk[0]
    for k in range(1, nx):
        key_sum = key_sum + send_sp(dk[-k % nx].astype(BF), k, 0).astype(F32)
    key_grad = key_sum.astype(BF)

    back = [parts[0]]
    for r in range(1, sp):
        dx, dc = r % nx, r // nx
        if dx and dc:
            back.append(send_sp(after(parts[r], v_got), -dx, dc))
        else:
            back.append(send_sp(parts[r], -dx, dc))
    input_grad = join_columns(idx, at_fwd, back, sp, dp, width)

    return (dq[None], key_grad[None], input_grad[None], weight_grad)


def solution(mesh):
    in_specs = (
        P("dp", "sp", None),
        P(("dp", "sp"), None),
        P("dp", "sp", None),
        P("dp", "sp", None),
        P("dp", "sp", None),
        P("dp", "sp"),
    )
    out_specs = (
        P("dp", "sp", None),
        P("dp", "sp", None),
        P("dp", "sp", None),
        P(("dp", "sp"), None),
    )
    return jax.shard_map(local, mesh=mesh, in_specs=in_specs, out_specs=out_specs, check_vma=False)
```

```python
import functools
import math

import jax
import jax.numpy as jnp
from jax import lax
from jax.experimental import pallas as pl
from jax.experimental.pallas import tpu as pltpu
from jax.sharding import PartitionSpec as P

HD = 128
NEG = -1e30
BF = jnp.bfloat16
F32 = jnp.float32
NT = (((1,), (1,)), ((), ()))
TN = (((0,), (0,)), ((), ()))
NN = (((1,), (0,)), ((), ()))
MIB = 1024 * 1024
VM = pl.BlockSpec(memory_space=pltpu.VMEM)
SM = pl.BlockSpec(memory_space=pltpu.SMEM)
HB = pl.BlockSpec(memory_space=pltpu.HBM)


def dot(a, b, dims):
    return lax.dot_general(a, b, dims, preferred_element_type=F32)


def ring_order(count):
    return list(range(0, count, 2)) + list(range(1, count, 2))[::-1]


def rows_at(index, size):
    return pl.ds(pl.multiple_of(index * size, size), size)


def grant(mib):
    return pltpu.CompilerParams(vmem_limit_bytes=mib * MIB)


def column_steps(dp, width):
    return max(1, min(4, dp * width // 128 // 2))


def piece_layout(sp, steps, cols):
    nx, out = sp // 2, []
    for r in range(sp):
        count = 2 if r % nx and r // nx and steps % 2 == 0 else 1
        out += [(r, i * cols // count, cols // count) for i in range(count)]
    return out


def fill_columns(layout, xs, x_hold, tok):
    for (r, at, size), x in zip(layout, xs):
        x_hold[r * tok : (r + 1) * tok, at : at + size] = x[...]


def split_kernel(sp, layout, steps, reps, width, base, idx_ref, x_ref, *rest):
    outs, (hold, part, sems) = rest[: len(layout)], rest[len(layout) :]
    block = reps * width
    copies = [
        pltpu.make_async_copy(
            x_ref.at[:, i * sp * block : (i + 1) * sp * block], hold.at[i], sems.at[i]
        )
        for i in range(steps)
    ]
    for copy in copies:
        copy.start()
    for i, copy in enumerate(copies):
        copy.wait()
        for a in range(sp):
            for d in range(reps):
                part[a, :, d * width : (d + 1) * width] = hold[
                    i, :, (d * sp + a) * width : (d * sp + a + 1) * width
                ]
        for (r, at, size), out in zip(layout, outs):
            if at <= i * block < at + size:
                out[:, i * block - at : (i + 1) * block - at] = part[idx_ref[base + r]]


def split_columns(idx, base, x, layout, sp, dp, width):
    tok = x.shape[0]
    steps = column_steps(dp, width)
    reps = dp // steps
    block = reps * width
    return pl.pallas_call(
        functools.partial(split_kernel, sp, layout, steps, reps, width, base),
        out_shape=[jax.ShapeDtypeStruct((tok, size), BF) for _, _, size in layout],
        in_specs=[SM, HB],
        out_specs=[VM] * len(layout),
        scratch_shapes=[
            pltpu.VMEM((steps, tok, sp * block), BF),
            pltpu.VMEM((sp, tok, block), BF),
            pltpu.SemaphoreType.DMA((steps,)),
        ],
        compiler_params=grant(12),
        cost_estimate=pl.CostEstimate(flops=0, bytes_accessed=4 * x.size, transcendentals=0),
        name="split_columns",
    )(idx, pltpu.with_memory_space_constraint(x, pltpu.HBM))


def join_kernel(sp, reps, width, base, idx_ref, *rest):
    ins, out, hold = rest[:sp], rest[sp], rest[sp + 1]
    block = reps * width
    at = pl.ds(pl.multiple_of(pl.program_id(0) * block, block), block)
    for r in range(sp):
        hold[idx_ref[base + r]] = ins[r][:, at]
    for a in range(sp):
        for d in range(reps):
            out[:, (d * sp + a) * width : (d * sp + a + 1) * width] = hold[
                a, :, d * width : (d + 1) * width
            ]


def join_columns(idx, base, pieces, sp, dp, width):
    tok = pieces[0].shape[0]
    steps = column_steps(dp, width)
    reps = dp // steps
    block = reps * width
    return pl.pallas_call(
        functools.partial(join_kernel, sp, reps, width, base),
        out_shape=jax.ShapeDtypeStruct((tok, sp * dp * width), BF),
        grid_spec=pltpu.PrefetchScalarGridSpec(
            num_scalar_prefetch=1,
            grid=(steps,),
            in_specs=[VM] * sp,
            out_specs=pl.BlockSpec((tok, sp * block), lambda d, _: (0, d)),
            scratch_shapes=[pltpu.VMEM((sp, tok, block), BF)],
        ),
        compiler_params=grant(12),
        cost_estimate=pl.CostEstimate(
            flops=0, bytes_accessed=4 * tok * sp * dp * width, transcendentals=0
        ),
        name="join_columns",
    )(idx, *pieces)


def block_kernel(tok, key_ref, doc_ref, out, docs, sems):
    keys = pltpu.make_async_copy(key_ref, out.at[0:tok, :], sems.at[0])
    ids = pltpu.make_async_copy(doc_ref, docs, sems.at[1])
    keys.start()
    ids.start()
    out[tok : tok + 16, :] = jnp.zeros((16, out.shape[1]), BF)
    ids.wait()
    out[tok : tok + 16, 0:tok] = jnp.broadcast_to(docs[...].astype(F32), (16, tok)).astype(BF)
    keys.wait()


def key_block(keys, docs):
    tok, kv = keys.shape
    return pl.pallas_call(
        functools.partial(block_kernel, tok),
        out_shape=jax.ShapeDtypeStruct((tok + 16, kv), BF),
        in_specs=[HB, HB],
        out_specs=VM,
        scratch_shapes=[pltpu.VMEM((1, tok), jnp.int32), pltpu.SemaphoreType.DMA((2,))],
        compiler_params=grant(4),
        cost_estimate=pl.CostEstimate(flops=0, bytes_accessed=4 * keys.size, transcendentals=0),
        name="key_block",
    )(
        pltpu.with_memory_space_constraint(keys, pltpu.HBM),
        pltpu.with_memory_space_constraint(docs, pltpu.HBM),
    )


def fill_keys(sp, tok, win, heads, idx_ref, kd_refs, key_hold, doc_hold, bias):
    first = jnp.maximum(idx_ref[0] + 1 - win, 0)
    head = pl.program_id(0)
    at = pl.ds(pl.multiple_of(head * HD, HD), HD)
    for r in range(sp):
        key_hold[rows_at(idx_ref[r], tok), :] = kd_refs[r][0:tok, at]

    @pl.when(head == 0)
    def _():
        for r in range(sp):
            doc_hold[idx_ref[r]] = kd_refs[r][tok : tok + 16, 0:tok].astype(F32)
        own = jnp.broadcast_to(doc_hold[idx_ref[0]][0:1, :], (tok, tok))
        query_at = idx_ref[0] * tok + lax.broadcasted_iota(jnp.int32, (tok, tok), 1)
        for b in range(win):
            docs = jnp.broadcast_to(doc_hold[first + b][0:1, :], (tok, tok)).T
            key_at = (first + b) * tok + lax.broadcasted_iota(jnp.int32, (tok, tok), 0)
            ok = (key_at <= query_at) & (docs == own)
            block = jnp.where(ok, F32(0.0), F32(NEG))
            for h in range(heads):
                bias[b * tok : (b + 1) * tok, h * tok : (h + 1) * tok] = block

    return first, at


def stack_heads(src, dst, tok, group):
    for h in range(group):
        dst[h * tok : (h + 1) * tok, :] = src[:, h * HD : (h + 1) * HD]


def emit_rel(acc, first, value, sp, tok, win, at, idx_ref, keep, send):
    nx = sp // 2
    acc[...] = jnp.zeros_like(acc)
    acc[pl.ds(pl.multiple_of(first * tok, tok), win * tok), :] = value
    for dx in range(nx):
        keep[dx, :, at] = acc[rows_at(idx_ref[dx], tok), :]
        send[dx, :, at] = acc[rows_at(idx_ref[nx + dx], tok), :]


def probs_kernel(sp, tok, win, group, pair, idx_ref, q_ref, g_ref, *rest):
    kds, (keep, send, lse_ref) = rest[:sp], rest[sp : sp + 3]
    key_hold, doc_hold, bias, q_st, g_st, p_st, acc = rest[sp + 3 :]
    first, cols = fill_keys(sp, tok, win, pair, idx_ref, kds, key_hold, doc_hold, bias)
    factor = F32(HD**-0.5 * math.log2(math.e))
    stack_heads(q_ref, q_st, tok, group)
    stack_heads(g_ref, g_st, tok, group)
    keys = key_hold[pl.ds(pl.multiple_of(first * tok, tok), win * tok), :]
    for h in range(0, group, pair):
        at = slice(h * tok, (h + pair) * tok)
        s = dot(keys, q_st[at, :], NT) * factor + bias[...]
        top = jnp.max(s, axis=0, keepdims=True)
        e = jnp.exp2(s - top)
        total = jnp.sum(e, axis=0, keepdims=True)
        p_st[:, at] = (e * (1.0 / total)).astype(BF)
        lse = top + jnp.log2(total)
        for i in range(pair):
            lse_ref[h + i : h + i + 1, :] = lse[:, i * tok : (i + 1) * tok]
    emit_rel(
        acc, first, dot(p_st[...], g_st[...], NN), sp, tok, win, cols, idx_ref, keep, send
    )


def probs_call(idx, q, g, kds, sp, tok, win, kvh, group):
    nx, seq, pair = sp // 2, sp * tok, 2
    part = jax.ShapeDtypeStruct((nx, tok, kvh * HD), F32)
    wide = pl.BlockSpec((tok, group * HD), lambda c, _: (0, c))
    return pl.pallas_call(
        functools.partial(probs_kernel, sp, tok, win, group, pair),
        out_shape=[part, part, jax.ShapeDtypeStruct((kvh * group, tok), F32)],
        grid_spec=pltpu.PrefetchScalarGridSpec(
            num_scalar_prefetch=1,
            grid=(kvh,),
            in_specs=[wide, wide] + [VM] * sp,
            out_specs=[VM, VM, pl.BlockSpec((group, tok), lambda c, _: (c, 0))],
            scratch_shapes=[
                pltpu.VMEM((seq, HD), BF),
                pltpu.VMEM((sp, 16, tok), F32),
                pltpu.VMEM((win * tok, pair * tok), F32),
                pltpu.VMEM((group * tok, HD), BF),
                pltpu.VMEM((group * tok, HD), BF),
                pltpu.VMEM((win * tok, group * tok), BF),
                pltpu.VMEM((seq, HD), F32),
            ],
        ),
        compiler_params=grant(20),
        cost_estimate=pl.CostEstimate(
            flops=4 * tok * win * tok * kvh * group * HD,
            bytes_accessed=8 * MIB,
            transcendentals=tok * win * tok * kvh * group,
        ),
        name="probs_dv",
    )(idx, q, g, *kds)


def scores_kernel(sp, tok, win, group, pair, idx_ref, q_ref, g_ref, lse_ref, v0_ref, v1_ref, *rest):
    nx = sp // 2
    kds, (dq_ref, keep, send) = rest[:sp], rest[sp : sp + 3]
    key_hold, doc_hold, bias, val_hold, q_st, g_st, ds_st, acc = rest[sp + 3 :]
    first, cols = fill_keys(sp, tok, win, pair, idx_ref, kds, key_hold, doc_hold, bias)
    for dx in range(nx):
        val_hold[rows_at(idx_ref[dx], tok), :] = v0_ref[dx, :, cols]
        val_hold[rows_at(idx_ref[nx + dx], tok), :] = v1_ref[dx, :, cols]
    scale = HD**-0.5
    factor = F32(scale * math.log2(math.e))
    stack_heads(q_ref, q_st, tok, group)
    stack_heads(g_ref, g_st, tok, group)
    window = pl.ds(pl.multiple_of(first * tok, tok), win * tok)
    keys, vals = key_hold[window, :], val_hold[window, :]
    for h in range(0, group, pair):
        at = slice(h * tok, (h + pair) * tok)
        lse = jnp.concatenate([lse_ref[h + i : h + i + 1, :] for i in range(pair)], axis=1)
        shift = lse - F32(math.log2(scale))
        s = dot(keys, q_st[at, :], NT) * factor + bias[...]
        scaled = jnp.exp2(s - shift)
        dp = dot(vals, g_st[at, :], NT)
        delta = jnp.sum(scaled * dp, axis=0, keepdims=True) * F32(1.0 / scale)
        ds_st[:, at] = (scaled * (dp - delta)).astype(BF)
    dq = dot(ds_st[...], keys, TN)
    for h in range(group):
        dq_ref[:, h * HD : (h + 1) * HD] = dq[h * tok : (h + 1) * tok, :].astype(BF)
    emit_rel(
        acc, first, dot(ds_st[...], q_st[...], NN), sp, tok, win, cols, idx_ref, keep, send
    )


def scores_call(idx, q, g, lse, v0, v1, kds, sp, tok, win, kvh, group):
    nx, seq, pair = sp // 2, sp * tok, 2
    part = jax.ShapeDtypeStruct((nx, tok, kvh * HD), F32)
    wide = pl.BlockSpec((tok, group * HD), lambda c, _: (0, c))
    return pl.pallas_call(
        functools.partial(scores_kernel, sp, tok, win, group, pair),
        out_shape=[jax.ShapeDtypeStruct(q.shape, BF), part, part],
        grid_spec=pltpu.PrefetchScalarGridSpec(
            num_scalar_prefetch=1,
            grid=(kvh,),
            in_specs=[wide, wide, pl.BlockSpec((group, tok), lambda c, _: (c, 0)), VM, VM]
            + [VM] * sp,
            out_specs=[wide, VM, VM],
            scratch_shapes=[
                pltpu.VMEM((seq, HD), BF),
                pltpu.VMEM((sp, 16, tok), F32),
                pltpu.VMEM((win * tok, pair * tok), F32),
                pltpu.VMEM((seq, HD), BF),
                pltpu.VMEM((group * tok, HD), BF),
                pltpu.VMEM((group * tok, HD), BF),
                pltpu.VMEM((win * tok, group * tok), BF),
                pltpu.VMEM((seq, HD), F32),
            ],
        ),
        compiler_params=grant(24),
        cost_estimate=pl.CostEstimate(
            flops=8 * tok * win * tok * kvh * group * HD,
            bytes_accessed=10 * MIB,
            transcendentals=tok * win * tok * kvh * group,
        ),
        name="scores_dq_dk",
    )(idx, q, g, lse, v0, v1, *kds)


def values_kernel(sp, dp, layout, tok, width, base, idx_ref, *rest):
    nx, count = sp // 2, len(layout)
    xs, ws = rest[:count], rest[count : count + dp]
    keep, send, x_hold, w_hold = rest[count + dp :]
    for i in range(dp):
        w_hold[rows_at(idx_ref[base + i], width), :] = ws[i][...]
    fill_columns(layout, xs, x_hold, tok)
    out = dot(x_hold[...], w_hold[...], NN)
    for dx in range(nx):
        keep[dx] = out[dx * tok : (dx + 1) * tok]
        send[dx] = out[(nx + dx) * tok : (nx + dx + 1) * tok]


def values_call(idx, base, xs, ws, layout, sp, dp, tok, width):
    nx, kv = sp // 2, ws[0].shape[1]
    cols = dp * width
    part = jax.ShapeDtypeStruct((nx, tok, kv), F32)
    return pl.pallas_call(
        functools.partial(values_kernel, sp, dp, layout, tok, width, base),
        out_shape=[part, part],
        in_specs=[SM] + [VM] * (len(xs) + dp),
        out_specs=[VM] * 2,
        scratch_shapes=[pltpu.VMEM((sp * tok, cols), BF), pltpu.VMEM((cols, kv), BF)],
        compiler_params=grant(16),
        cost_estimate=pl.CostEstimate(
            flops=2 * sp * tok * cols * kv, bytes_accessed=8 * MIB, transcendentals=0
        ),
        name="values_part",
    )(idx, *xs, *ws)


def wgrad_kernel(sp, nz, ny, layout, tok, width, base, idx_ref, *rest):
    nx, count = sp // 2, len(layout)
    xs, (g0, g1) = rest[:count], rest[count : count + 2]
    outs = rest[count + 2 : count + 2 + 2 * nz]
    x_hold, g_hold, total = rest[count + 2 + 2 * nz :]
    fill_columns(layout, xs, x_hold, tok)
    for dx in range(nx):
        for core, src in ((0, g0), (1, g1)):
            r = core * nx + dx
            g_hold[r * tok : (r + 1) * tok, :] = src[dx]
    cols = x_hold.shape[1]
    step = min(cols, 512)
    for at in range(0, cols, step):
        total[at : at + step, :] = dot(x_hold[:, at : at + step], g_hold[...], TN)
    for k in range(nz):
        outs[k][...] = total[rows_at(idx_ref[base + k * ny], width), :].astype(BF)
        for j in range(1, ny):
            outs[nz + k][j - 1] = total[rows_at(idx_ref[base + k * ny + j], width), :]


def wgrad_call(idx, base, xs, g0, g1, layout, sp, nz, ny, tok, width):
    kv = g0.shape[2]
    cols = nz * ny * width
    return pl.pallas_call(
        functools.partial(wgrad_kernel, sp, nz, ny, layout, tok, width, base),
        out_shape=[jax.ShapeDtypeStruct((width, kv), BF)] * nz
        + [jax.ShapeDtypeStruct((ny - 1, width, kv), F32)] * nz,
        in_specs=[SM] + [VM] * (len(xs) + 2),
        out_specs=[VM] * (2 * nz),
        scratch_shapes=[
            pltpu.VMEM((sp * tok, cols), BF),
            pltpu.VMEM((sp * tok, kv), BF),
            pltpu.VMEM((cols, kv), F32),
        ],
        compiler_params=grant(20),
        cost_estimate=pl.CostEstimate(
            flops=2 * sp * tok * cols * kv, bytes_accessed=7 * MIB, transcendentals=0
        ),
        name="weight_grad_part",
    )(idx, *xs, g0, g1)


def igrad_kernel(sp, dp, tok, width, base, idx_ref, g0, g1, *rest):
    nx = sp // 2
    ws, outs = rest[:dp], rest[dp : dp + sp]
    g_hold, w_hold = rest[dp + sp :]
    for i in range(dp):
        w_hold[rows_at(idx_ref[base + i], width), :] = ws[i][...]
    for dx in range(nx):
        g_hold[dx * tok : (dx + 1) * tok, :] = g0[dx]
        g_hold[(nx + dx) * tok : (nx + dx + 1) * tok, :] = g1[dx]
    cols = w_hold.shape[0]
    step = min(cols, 512)
    for at in range(0, cols, step):
        out = dot(g_hold[...], w_hold[at : at + step, :], NT)
        for r in range(sp):
            outs[r][:, at : at + step] = out[r * tok : (r + 1) * tok].astype(BF)


def igrad_call(idx, base, g0, g1, ws, sp, dp, tok, width):
    kv = g0.shape[2]
    cols = dp * width
    return pl.pallas_call(
        functools.partial(igrad_kernel, sp, dp, tok, width, base),
        out_shape=[jax.ShapeDtypeStruct((tok, cols), BF)] * sp,
        in_specs=[SM] + [VM] * (2 + dp),
        out_specs=[VM] * sp,
        scratch_shapes=[pltpu.VMEM((sp * tok, kv), BF), pltpu.VMEM((cols, kv), BF)],
        compiler_params=grant(16),
        cost_estimate=pl.CostEstimate(
            flops=2 * sp * tok * cols * kv, bytes_accessed=5 * MIB, transcendentals=0
        ),
        name="input_grad_part",
    )(idx, g0, g1, *ws)


def after(value, *others):
    return lax.optimization_barrier((value, *others))[0]


def local(layer_input, value_weight, query_states, key_states, out_grad, doc_ids):
    sp, dp = lax.axis_size("sp"), lax.axis_size("dp")
    nx = sp // 2
    ny = max(1, min(nx, dp))
    nz = dp // ny
    tok = layer_input.shape[1]
    width = value_weight.shape[0]
    kvh = key_states.shape[2] // HD
    group = query_states.shape[2] // HD // kvh
    win = min(sp, sp // 2 + 1)

    def sp_perm(dx, dc):
        return [(i, ((i // 2 + dx) % nx) * 2 + (i % 2 ^ dc)) for i in range(sp)]

    def send_sp(v, dx, dc):
        return lax.ppermute(v, "sp", sp_perm(dx % nx, dc))

    z_ring, y_ring = ring_order(nz), ring_order(ny)

    def pred(ring, at, k):
        return ring[(ring.index(at) - k) % len(ring)]

    z_next = [
        (z_ring[p] * ny + y, z_ring[(p + 1) % nz] * ny + y) for p in range(nz) for y in range(ny)
    ]
    z_back = [(j, i) for i, j in z_next]
    ahead = nz // 2
    behind = nz - 1 - ahead
    y_next = [
        (z * ny + y_ring[p], z * ny + y_ring[(p + 1) % ny]) for p in range(ny) for z in range(nz)
    ]

    def send_z(v, forward=True):
        return lax.ppermute(v, "dp", z_next if forward else z_back)

    def send_y(v):
        return lax.ppermute(v, "dp", y_next)

    from_z = [0, *range(1, ahead + 1), *(-k for k in range(1, behind + 1))]
    to_z = sorted(from_z, key=lambda k: (-abs(k), -k))

    table = []
    for d in range(dp):
        z, y = d // ny, d % ny
        for s in range(sp):
            x, core = s // 2, s % 2
            row = [((x - dx) % nx) * 2 + (core ^ dc) for dc in range(2) for dx in range(nx)]
            row += [((x + dx) % nx) * 2 + (core ^ dc) for dc in range(2) for dx in range(nx)]
            row += [
                pred(z_ring, z, k) * ny + pred(y_ring, y, j) for k in from_z for j in range(ny)
            ]
            row += [
                pred(z_ring, z, -k) * ny + pred(y_ring, y, j)
                for k in to_z
                for j in range(1, ny + 1)
            ]
            table.append(row)
    at_fwd, at_gather, at_scatter = sp, 2 * sp, 2 * sp + dp
    flat = lax.axis_index("dp") * sp + lax.axis_index("sp")
    idx = lax.dynamic_index_in_dim(jnp.asarray(table, jnp.int32), flat, 0, keepdims=False)

    q, g = query_states[0], out_grad[0]

    kd = key_block(key_states[0], doc_ids)
    near = [kd] + [send_sp(kd, dx, 0) for dx in range(1, nx)]
    kds = near + [send_sp(v, 0, 1) for v in near]

    z_rows = [value_weight]
    for _ in range(1, ahead + 1):
        z_rows.append(send_z(z_rows[-1]))
    for k in range(1, behind + 1):
        z_rows.append(send_z(z_rows[-1] if k > 1 else value_weight, False))
    rows = []
    for v in z_rows:
        for j in range(ny):
            rows.append(v)
            if j + 1 < ny:
                v = send_y(v)

    layout = piece_layout(sp, column_steps(dp, width), dp * width)
    pieces = split_columns(idx, at_fwd, layer_input[0], layout, sp, dp, width)
    ready = [pieces[0]] + [after(v, near[-1]) for v in pieces[1:]]

    dv_keep, dv_send, lse = probs_call(idx, q, g, kds, sp, tok, win, kvh, group)

    def reduce_core(keep, send):
        return keep + send_sp(send, 0, 1)

    def reduce_all(keep, send):
        here = reduce_core(keep, send)
        small = here.astype(BF)
        total, got = here, small
        for k in range(1, nx):
            got = send_sp(small, k, 0)
            total = total + jnp.roll(got, k, axis=0).astype(F32)
        mine = total.astype(BF)
        return mine, send_sp(mine, 0, 1), got

    vg0, vg1, vg_got = reduce_all(dv_keep, dv_send)

    xs = [pieces[0]]
    for (r, at, _), v in list(zip(layout, ready))[1:]:
        dx, dc = r % nx, r // nx
        xs.append(send_sp(after(v, vg_got) if at else v, dx, dc))

    parts = igrad_call(idx, at_gather, vg0, vg1, rows, sp, dp, tok, width)

    blocks = wgrad_call(idx, at_scatter, xs, vg0, vg1, layout, sp, nz, ny, tok, width)
    lines = {}
    for i, k in enumerate(to_z):
        line = blocks[i]
        for j in range(1, ny):
            line = send_y(line.astype(BF)).astype(F32) + blocks[nz + i][j - 1]
        lines[k] = line.astype(F32)
    weight_grad = lines[0]
    for count, sign in ((ahead, 1), (behind, -1)):
        run = None
        for k in range(count, 0, -1):
            run = lines[sign * k] if run is None else run + lines[sign * k]
            run = send_z(run.astype(BF), sign > 0).astype(F32)
        if run is not None:
            weight_grad = weight_grad + run

    v_keep, v_send = values_call(idx, at_gather, xs, rows, layout, sp, dp, tok, width)
    v0, v1, v_got = reduce_all(v_keep, v_send)
    dq, dk_keep, dk_send = scores_call(idx, q, g, lse, v0, v1, kds, sp, tok, win, kvh, group)
    dk = reduce_core(dk_keep, dk_send)
    key_sum = dk[0]
    for k in range(1, nx):
        key_sum = key_sum + send_sp(dk[-k % nx].astype(BF), k, 0).astype(F32)
    key_grad = key_sum.astype(BF)

    back = [parts[0]]
    for r in range(1, sp):
        dx, dc = r % nx, r // nx
        if dx and dc:
            back.append(send_sp(after(parts[r], v_got), -dx, dc))
        else:
            back.append(send_sp(parts[r], -dx, dc))
    input_grad = join_columns(idx, at_fwd, back, sp, dp, width)

    return (dq[None], key_grad[None], input_grad[None], weight_grad)


def solution(mesh):
    in_specs = (
        P("dp", "sp", None),
        P(("dp", "sp"), None),
        P("dp", "sp", None),
        P("dp", "sp", None),
        P("dp", "sp", None),
        P("dp", "sp"),
    )
    out_specs = (
        P("dp", "sp", None),
        P("dp", "sp", None),
        P("dp", "sp", None),
        P(("dp", "sp"), None),
    )
    return jax.shard_map(local, mesh=mesh, in_specs=in_specs, out_specs=out_specs, check_vma=False)
```
